128 devices in a mesh: energy: 32 (over x, z_lo, y), slab: 4 (over z_hi, core).
Axes of the slice: x: 4, y: 4, z: 4 (z_hi: 2, z_lo: 2; z = z_hi * 2 + z_lo), core: 2. Of those that a mesh axis runs over, the one named last changes fastest.
Arguments:
- green_diag: float32 [4, 1024, 2, 128, 128], P('slab', 'energy'), may hold values from -0.375 to 0.375
- green_lower: float32 [4, 1024, 2, 128, 128], P('slab', 'energy'), may hold values from -0.375 to 0.375
- green_upper: float32 [4, 1024, 2, 128, 128], P('slab', 'energy'), may hold values from -0.375 to 0.375
- sigma_lesser: float32 [4, 1024, 2, 128, 128], P('slab', 'energy'), may hold values from -6 to 6
- screened: float32 [4, 1024, 2, 128, 128], P('slab', None, None, 'energy'), may hold values from -6 to 6
- pattern: int32 [4, 128], P('slab'), may hold values 0 or 1
Outputs:
- green_lesser: float32 [4, 1024, 2, 128, 128], P('slab', 'energy')
The draws below stay inside these ranges and needn't reach their ends.
All inputs are finite; a program needn't handle non-finite values. No bound on the sum of `pattern` on one device may be relied on, other than what follows from the above.
Results may differ from the reference program's by a relative error of at most 0.0001.
Values sent between devices are 32-bit elements; how exact they have to be, the bound alone decides.
A program may use at most 128 MiB of HBM per device.

```python
import jax
import jax.numpy as jnp
from jax import lax

B = 128
E = 1024
NBLK = 4


def with_ends(drawn, own_key, low, largest):
    dims = drawn.shape
    place = [jax.random.randint(jax.random.fold_in(own_key, axis), (), 0, dims[axis]) for axis in range(len(dims))]
    drawn = drawn.at[tuple(place)].set(low)
    longest = dims.index(max(dims))
    place[longest] = (place[longest] + 1) % dims[longest]
    return drawn.at[tuple(place)].set(largest)


def level_of(rng, shape, shards, least, largest):
    factor_of = 1.0
    for axis_at, blocks in shards:
        draws = jax.random.uniform(jax.random.fold_in(jax.random.fold_in(rng, 6), axis_at), (blocks,), jnp.float32, least / len(shards), largest / len(shards))
        factor_of = factor_of * jnp.repeat(jnp.exp(draws), shape[axis_at] // blocks).reshape((-1,) + (1,) * (len(shape) - 1 - axis_at))
    return factor_of


def normal_values(stream_key, shape, spread, reach, shards=(), kind=jnp.bfloat16):
    gain = level_of(stream_key, shape, shards, -0.22, 0.18) if shards else 1.0
    values = jax.random.normal(stream_key, shape, jnp.float32) * spread * gain
    return jnp.minimum(jnp.maximum(values, -reach), reach).astype(kind)


def setup_inputs(seed: int = 0) -> dict:
    key_list = jax.random.split(jax.random.key(seed), 7)
    return {
        "green_diag": normal_values(key_list[0], (NBLK, E, 2, B, B), (2 * B) ** -0.5, 0.375, ((0, 4), (1, 32)), jnp.float32),
        "green_lower": normal_values(key_list[1], (NBLK, E, 2, B, B), (2 * B) ** -0.5, 0.375, ((0, 4), (1, 32)), jnp.float32),
        "green_upper": normal_values(key_list[2], (NBLK, E, 2, B, B), (2 * B) ** -0.5, 0.375, ((0, 4), (1, 32)), jnp.float32),
        "sigma_lesser": normal_values(key_list[3], (NBLK, E, 2, B, B), 1.0, 6.0, ((0, 4), (1, 32)), jnp.float32),
        "screened": normal_values(key_list[4], (NBLK, E, 2, B, B), 1.0, 6.0, ((0, 4), (3, 32)), jnp.float32),
        "pattern": with_ends((jax.random.randint(key_list[5], (NBLK, B), 0, 2) < 1).astype(jnp.int32), jax.random.fold_in(key_list[5], 1), 0, 1),
    }


def matmul_plain(first_op, second_op):
    return jnp.einsum("...ab,...bc->...ac", first_op, second_op, precision=lax.Precision.HIGHEST)


def matmul_adjoint(first_op, second_op):
    return jnp.einsum("...ab,...cb->...ac", first_op, second_op, precision=lax.Precision.HIGHEST)


def sandwich(outer_factor, middle_factor):
    outer_real = outer_factor[..., 0, :, :]
    outer_imag = outer_factor[..., 1, :, :]
    middle_real = middle_factor[..., 0, :, :]
    middle_imag = middle_factor[..., 1, :, :]
    prod_real = matmul_plain(outer_real, middle_real) - matmul_plain(outer_imag, middle_imag)
    prod_imag = matmul_plain(outer_real, middle_imag) + matmul_plain(outer_imag, middle_real)
    final_real = matmul_adjoint(prod_real, outer_real) + matmul_adjoint(prod_imag, outer_imag)
    final_imag = matmul_adjoint(prod_imag, outer_real) - matmul_adjoint(prod_real, outer_imag)
    return jnp.stack([final_real, final_imag], axis=-3)


def lesser_product(green_diag, green_lower, green_upper, sigma_blocks):
    block_count = sigma_blocks.shape[0]
    results = []
    for index in range(block_count):
        total = sandwich(green_diag[index], sigma_blocks[index])
        if index > 0:
            total = total + sandwich(green_lower[index], sigma_blocks[index - 1])
        if index + 1 < block_count:
            total = total + sandwich(green_upper[index], sigma_blocks[index + 1])
        results.append(total)
    return jnp.stack(results, axis=0)


def reference(green_diag, green_lower, green_upper, sigma_lesser, screened, pattern):
    first_pass = lesser_product(green_diag, green_lower, green_upper, sigma_lesser)
    updated = []
    for index in range(first_pass.shape[0]):
        values = lax.complex(first_pass[index, :, 0], first_pass[index, :, 1])
        spectrum = jnp.fft.fft(values, axis=0)
        weights = lax.complex(screened[index, :, 0], screened[index, :, 1])
        convolved = jnp.fft.ifft(spectrum * weights, axis=0)
        scatter_part = jnp.stack([-jnp.imag(convolved), jnp.real(convolved)], axis=1)
        mask_float = pattern[index].astype(jnp.float32)
        kept = mask_float[:, None] * mask_float[None, :]
        updated.append(sigma_lesser[index] + kept[None, None] * scatter_part)
    sigma_new = jnp.stack(updated, axis=0)
    return lesser_product(green_diag, green_lower, green_upper, sigma_new)
```

```python
import functools
import math

import jax
import jax.numpy as jnp
import numpy as np
from jax import lax
from jax.experimental import pallas as pl
from jax.experimental.pallas import tpu as pltpu
from jax.sharding import PartitionSpec as P

BF = jnp.bfloat16
F32 = jnp.float32
B = 128
LIMIT = 60 << 20


def split(x):
    h=x.astype(BF); return h,(x-h.astype(F32)).astype(BF)
def rot(h):
    return jnp.concatenate([h, jnp.concatenate([-h[:,128:], h[:,:128]],1)],0)
def dot(a,b): return lax.dot_general(a,b,(((1,),(0,)),((),())),preferred_element_type=F32)
def dott(a,b): return lax.dot_general(a,b,(((1,),(1,)),((),())),preferred_element_type=F32)
def rotT(Tr,Ti):
    return jnp.concatenate([jnp.concatenate([Tr,-Ti],1),jnp.concatenate([Ti,Tr],1)],0)
def term(G,S):
    Gh,Gl=split(jnp.concatenate([G[0],G[1]],1)); Sh,Sl=split(jnp.concatenate([S[0],S[1]],1))
    tr,ti=G[0].T,G[1].T
    trh,trl=split(tr); tih,til=split(ti)
    Wh=rotT(trh,tih); Wl=rotT(trl,til)
    T2=dot(jnp.concatenate([Gh,Gl],0),rot(Sh)); T=T2[:128]+T2[128:]+dot(Gh,rot(Sl))
    Th,Tl=split(T)
    F2=dot(jnp.concatenate([Th,Tl],0),Wh)
    return F2[:128]+F2[128:]+dot(Th,Wl)

def dft_mats():
    a=np.arange(128); th=2*np.pi*((a[:,None]*a[None,:])%128)/128
    C,S=np.cos(th),np.sin(th)
    f=np.block([[C,S],[-S,C]]); b=np.block([[C,-S],[S,C]])
    out=[]
    for m in (f,b):
        h=m.astype(np.float32).astype(BF); l=(m-h.astype(np.float64)).astype(np.float32).astype(BF)
        out.append(np.concatenate([h,l],0))
    return np.stack(out)
def tw_tab():
    a=np.arange(128)[:,None]; p=np.arange(8)[None,:]
    th=2*np.pi*(a*p)/1024
    t=np.zeros((128,128),np.float32); t[:,:8]=np.cos(th); t[:,8:16]=np.sin(th)
    return t

R2=math.sqrt(0.5)
def radix8(x,sign):
    add=lambda u,v:(u[0]+v[0],u[1]+v[1]); sub=lambda u,v:(u[0]-v[0],u[1]-v[1])
    mi=(lambda u:(u[1],-u[0])) if sign<0 else (lambda u:(-u[1],u[0]))
    def r4(y):
        s0,d0=add(y[0],y[2]),sub(y[0],y[2]); s1,d1=add(y[1],y[3]),mi(sub(y[1],y[3]))
        return [add(s0,s1),add(d0,d1),sub(s0,s1),sub(d0,d1)]
    e=r4(x[0::2]); o=r4(x[1::2])
    def w1(u):
        m=mi(u); return ((u[0]+m[0])*R2,(u[1]+m[1])*R2)
    o=[o[0],w1(o[1]),mi(o[2]),w1(mi(o[3]))]
    return [add(e[k],o[k]) for k in range(4)]+[sub(e[k],o[k]) for k in range(4)]
def conv_r(ld_x,ld_s,st_o,tw,dm,yh,yl,v):
    for ch in range(8):
        x=[(ld_x(4*b+ch//2,0,(ch%2)*16),ld_x(4*b+ch//2,1,(ch%2)*16)) for b in range(8)]
        y=radix8(x,-1)
        rs=slice(ch*16,ch*16+16)
        for p in range(8):
            re,im=y[p]
            if p:
                c,s=tw[p,0,rs,:],tw[p,1,rs,:]
                re,im=re*c+im*s,im*c-re*s
            for k,val in enumerate((re,im)):
                h,l=split(val)
                yh[p,k*128+ch*16:k*128+ch*16+16,:]=h; yl[p,k*128+ch*16:k*128+ch*16+16,:]=l
    for pp in range(4):
        p0,p1=2*pp,2*pp+1
        H=jnp.concatenate([yh[p0],yh[p1]],1); L=jnp.concatenate([yl[p0],yl[p1]],1)
        D=dm[0]
        A=dot(D,H); Z=A[:256]+A[256:]+dot(D[:256],L)
        wr=jnp.concatenate([ld_s(p0,0),ld_s(p1,0)],1); wi=jnp.concatenate([ld_s(p0,1),ld_s(p1,1)],1)
        zr,zi=Z[:128],Z[128:]
        Q=jnp.concatenate([zr*wr-zi*wi,zr*wi+zi*wr],0)
        h,l=split(Q)
        D=dm[1]
        A=dot(D,h); V=A[:256]+A[256:]+dot(D[:256],l)
        v[p0]=V[:,:128]; v[p1]=V[:,128:]
    for ch in range(16):
        rs=slice(ch*8,ch*8+8); ri=slice(128+ch*8,128+ch*8+8)
        x=[]
        for p in range(8):
            re,im=v[p,rs,:],v[p,ri,:]
            if p:
                c,s=tw[p,0,rs,:],tw[p,1,rs,:]
                re,im=re*c-im*s,im*c+re*s
            x.append((re,im))
        y=radix8(x,1)
        for b in range(8):
            d=4*b+ch//4
            st_o(d,0,(ch%4)*8,y[b][1]*(-1.0/1024)); st_o(d,1,(ch%4)*8,y[b][0]*(1.0/1024))
def fill_tw(tab,tw):
    for p in range(1,8):
        tw[p,0]=jnp.broadcast_to(tab[:,p:p+1],(128,128)); tw[p,1]=jnp.broadcast_to(tab[:,8+p:9+p],(128,128))

E_BLOCK = 4


def diag_kernel(g, s, out):
    for k in range(E_BLOCK):
        f = term(g[k], s[k])
        out[k, 0] = f[:, :B]
        out[k, 1] = f[:, B:]


def side_kernel(spread, gl, gu, sb, sa, base, out):
    i = pl.program_id(0)
    for k in range(E_BLOCK):
        f = term(gl[k], sb[k]) + term(gu[k], sa[k])
        re = f[:, :B] + base[k, 0]
        im = f[:, B:] + base[k, 1]
        if spread:
            e = i * E_BLOCK + k
            out[pl.ds(e, B, stride=64), :] = re
            out[pl.ds(32 + e, B, stride=64), :] = im
        else:
            out[k, 0] = re
            out[k, 1] = im


def renew_kernel(sigma, conv, kept, out):
    i = pl.program_id(0)
    for k in range(E_BLOCK):
        e = i * E_BLOCK + k
        mask = kept[...]
        out[k, 0] = sigma[k, 0] + mask * conv[pl.ds(e, B, stride=64), :]
        out[k, 1] = sigma[k, 1] + mask * conv[pl.ds(32 + e, B, stride=64), :]


def conv_kernel(x, sc, dm, tab, o, tw, yh, yl, v):
    r = pl.program_id(0)

    @pl.when(r == 0)
    def _():
        fill_tw(tab, tw)

    def ld_x(s, c, r0):
        return x[s, 0, c, r0 : r0 + 16, :]

    def ld_s(p, c):
        return sc[pl.ds(p * 8 + c * 4 + r, 128, stride=64), :]

    def st_o(d, c, r0, val):
        o[d, 0, c, r0 : r0 + 8, :] = val

    conv_r(ld_x, ld_s, st_o, tw, dm, yh, yl, v)


def full(shape):
    return pl.BlockSpec(shape, lambda i: (0,) * len(shape))


PARAMS = pltpu.CompilerParams(vmem_limit_bytes=LIMIT)
E_SPEC = pl.BlockSpec((E_BLOCK, 2, B, B), lambda i: (i, 0, 0, 0))
FIELD = jax.ShapeDtypeStruct((32, 2, B, B), F32)
MOVED = jax.ShapeDtypeStruct((8192, B), F32)


def cost(terms):
    return pl.CostEstimate(flops=terms * 32 * 100_000_000, bytes_accessed=terms * 12_000_000, transcendentals=0)


def lesser_product(gd, gl, gu, sigma, spread):
    before = lax.ppermute(sigma, "slab", [(i, i + 1) for i in range(3)])
    after = lax.ppermute(sigma, "slab", [(i + 1, i) for i in range(3)])
    grid = (32 // E_BLOCK,)
    base = pl.pallas_call(
        diag_kernel, grid=grid, in_specs=[E_SPEC] * 2, out_specs=E_SPEC, out_shape=FIELD,
        compiler_params=PARAMS, cost_estimate=cost(1), name="diag",
    )(gd, sigma)
    return pl.pallas_call(
        functools.partial(side_kernel, spread), grid=grid, in_specs=[E_SPEC] * 5,
        out_specs=full((8192, B)) if spread else E_SPEC, out_shape=MOVED if spread else FIELD,
        compiler_params=PARAMS, cost_estimate=cost(2), name="sides",
    )(gl, gu, before, after, base)


def convolve(x, sc):
    bs = pl.BlockSpec((32, 1, 2, 32, B), lambda i: (0, i, 0, 0, 0))
    return pl.pallas_call(
        conv_kernel, grid=(4,),
        in_specs=[bs, full((8192, B)), full((2, 512, 256)), full((B, B))], out_specs=bs,
        out_shape=jax.ShapeDtypeStruct((32, 4, 2, 32, B), F32),
        scratch_shapes=[
            pltpu.VMEM((8, 2, B, B), F32), pltpu.VMEM((8, 256, B), BF),
            pltpu.VMEM((8, 256, B), BF), pltpu.VMEM((8, 256, B), F32),
        ],
        compiler_params=PARAMS, name="convolve",
    )(x, sc, jnp.asarray(dft_mats()), jnp.asarray(tw_tab()))


def local(green_diag, green_lower, green_upper, sigma_lesser, screened, pattern):
    gd, gl, gu, sigma = green_diag[0], green_lower[0], green_upper[0], sigma_lesser[0]
    first = lesser_product(gd, gl, gu, sigma, True).reshape(32, 4, 2, 32, B)
    moved = lax.all_to_all(first, "energy", split_axis=0, concat_axis=0, tiled=True)
    interaction = convolve(moved, screened.reshape(8192, B))
    returned = lax.all_to_all(interaction, "energy", split_axis=0, concat_axis=0, tiled=True)
    mask = pattern[0].astype(F32)
    kept = mask[:, None] * mask[None, :]
    sigma_new = pl.pallas_call(
        renew_kernel, grid=(32 // E_BLOCK,), in_specs=[E_SPEC, full((8192, B)), full((B, B))],
        out_specs=E_SPEC, out_shape=FIELD, compiler_params=PARAMS, name="renew",
    )(sigma, returned.reshape(8192, B), kept)
    return lesser_product(gd, gl, gu, sigma_new, False)[None]


def solution(mesh):
    return jax.shard_map(
        local,
        mesh=mesh,
        in_specs=(
            P("slab", "energy", None, None, None),
            P("slab", "energy", None, None, None),
            P("slab", "energy", None, None, None),
            P("slab", "energy", None, None, None),
            P("slab", None, None, "energy", None),
            P("slab", None),
        ),
        out_specs=P("slab", "energy", None, None, None),
        check_vma=False,
    )
```

```python
import functools
import math

import jax
import jax.numpy as jnp
import numpy as np
from jax import lax
from jax.experimental import pallas as pl
from jax.experimental.pallas import tpu as pltpu
from jax.sharding import PartitionSpec as P

BF = jnp.bfloat16
F32 = jnp.float32
B = 128
LIMIT = 60 << 20


def split(x):
    h=x.astype(BF); return h,(x-h.astype(F32)).astype(BF)
def rot(h):
    return jnp.concatenate([h, jnp.concatenate([-h[:,128:], h[:,:128]],1)],0)
def dot(a,b): return lax.dot_general(a,b,(((1,),(0,)),((),())),preferred_element_type=F32)
def dott(a,b): return lax.dot_general(a,b,(((1,),(1,)),((),())),preferred_element_type=F32)
def rotT(Tr,Ti):
    return jnp.concatenate([jnp.concatenate([Tr,-Ti],1),jnp.concatenate([Ti,Tr],1)],0)
def term(G,S):
    Gh,Gl=split(jnp.concatenate([G[0],G[1]],1)); Sh,Sl=split(jnp.concatenate([S[0],S[1]],1))
    tr,ti=G[0].T,G[1].T
    trh,trl=split(tr); tih,til=split(ti)
    Wh=rotT(trh,tih); Wl=rotT(trl,til)
    T2=dot(jnp.concatenate([Gh,Gl],0),rot(Sh)); T=T2[:128]+T2[128:]+dot(Gh,rot(Sl))
    Th,Tl=split(T)
    F2=dot(jnp.concatenate([Th,Tl],0),Wh)
    return F2[:128]+F2[128:]+dot(Th,Wl)

def dft_mats():
    a=np.arange(128); th=2*np.pi*((a[:,None]*a[None,:])%128)/128
    C,S=np.cos(th),np.sin(th)
    f=np.block([[C,S],[-S,C]]); b=np.block([[C,-S],[S,C]])
    out=[]
    for m in (f,b):
        h=m.astype(np.float32).astype(BF); l=(m-h.astype(np.float64)).astype(np.float32).astype(BF)
        out.append(np.concatenate([h,l],0))
    return np.stack(out)
def tw_tab():
    a=np.arange(128)[:,None]; p=np.arange(8)[None,:]
    th=2*np.pi*(a*p)/1024
    t=np.zeros((128,128),np.float32); t[:,:8]=np.cos(th); t[:,8:16]=np.sin(th)
    return t

R2=math.sqrt(0.5)
def radix8(x,sign):
    add=lambda u,v:(u[0]+v[0],u[1]+v[1]); sub=lambda u,v:(u[0]-v[0],u[1]-v[1])
    mi=(lambda u:(u[1],-u[0])) if sign<0 else (lambda u:(-u[1],u[0]))
    def r4(y):
        s0,d0=add(y[0],y[2]),sub(y[0],y[2]); s1,d1=add(y[1],y[3]),mi(sub(y[1],y[3]))
        return [add(s0,s1),add(d0,d1),sub(s0,s1),sub(d0,d1)]
    e=r4(x[0::2]); o=r4(x[1::2])
    def w1(u):
        m=mi(u); return ((u[0]+m[0])*R2,(u[1]+m[1])*R2)
    o=[o[0],w1(o[1]),mi(o[2]),w1(mi(o[3]))]
    return [add(e[k],o[k]) for k in range(4)]+[sub(e[k],o[k]) for k in range(4)]
def conv_r(ld_x,ld_s,st_o,tw,dm,yh,yl,v):
    for ch in range(8):
        x=[(ld_x(4*b+ch//2,0,(ch%2)*16),ld_x(4*b+ch//2,1,(ch%2)*16)) for b in range(8)]
        y=radix8(x,-1)
        rs=slice(ch*16,ch*16+16)
        for p in range(8):
            re,im=y[p]
            if p:
                c,s=tw[p,0,rs,:],tw[p,1,rs,:]
                re,im=re*c+im*s,im*c-re*s
            for k,val in enumerate((re,im)):
                h,l=split(val)
                yh[p,k*128+ch*16:k*128+ch*16+16,:]=h; yl[p,k*128+ch*16:k*128+ch*16+16,:]=l
    for pp in range(4):
        p0,p1=2*pp,2*pp+1
        H=jnp.concatenate([yh[p0],yh[p1]],1); L=jnp.concatenate([yl[p0],yl[p1]],1)
        D=dm[0]
        A=dot(D,H); Z=A[:256]+A[256:]+dot(D[:256],L)
        wr=jnp.concatenate([ld_s(p0,0),ld_s(p1,0)],1); wi=jnp.concatenate([ld_s(p0,1),ld_s(p1,1)],1)
        zr,zi=Z[:128],Z[128:]
        Q=jnp.concatenate([zr*wr-zi*wi,zr*wi+zi*wr],0)
        h,l=split(Q)
        D=dm[1]
        A=dot(D,h); V=A[:256]+A[256:]+dot(D[:256],l)
        v[p0]=V[:,:128]; v[p1]=V[:,128:]
    for ch in range(16):
        rs=slice(ch*8,ch*8+8); ri=slice(128+ch*8,128+ch*8+8)
        x=[]
        for p in range(8):
            re,im=v[p,rs,:],v[p,ri,:]
            if p:
                c,s=tw[p,0,rs,:],tw[p,1,rs,:]
                re,im=re*c-im*s,im*c+re*s
            x.append((re,im))
        y=radix8(x,1)
        for b in range(8):
            d=4*b+ch//4
            st_o(d,0,(ch%4)*8,y[b][1]*(-1.0/1024)); st_o(d,1,(ch%4)*8,y[b][0]*(1.0/1024))
def fill_tw(tab,tw):
    for p in range(1,8):
        tw[p,0]=jnp.broadcast_to(tab[:,p:p+1],(128,128)); tw[p,1]=jnp.broadcast_to(tab[:,8+p:9+p],(128,128))

ENERGY = 32
ROWS = 8192
CHUNK = 2048
UNROLL = 4
MESH = pl.DeviceIdType.MESH


def kernel(
    gd_h, gl_h, gu_h, s_h, sc_h, kept, dm, tab, out_h,
    gd, gl, gu, sig, bef, aft, obuf, recv, ret, scr, tw, yh, yl, v,
    load_sem, sc_sem, own_sem, out_sem, up_s, down_s, up_r, down_r,
    a_s, a_r, b_s, b_r, up2_s, down2_s, up2_r, down2_r, credit,
):
    me = lax.axis_index("energy")
    slab = lax.axis_index("slab")
    first, last = slab == 0, slab == 3

    def loads(k):
        at = pl.ds(k * CHUNK, CHUNK)
        return [
            pltpu.make_async_copy(src.at[at], dst.at[at], load_sem.at[j, k])
            for j, (src, dst) in enumerate(((s_h, sig), (gd_h, gd), (gl_h, gl), (gu_h, gu)))
        ]

    sc_copy = pltpu.make_async_copy(sc_h, scr, sc_sem.at[0])
    for k in range(4):
        for c in loads(k):
            c.start()
    sc_copy.start()

    barrier = pltpu.get_barrier_semaphore()

    def greet(d, carry):
        pl.semaphore_signal(barrier, inc=1, device_id={"energy": lax.rem(me + d, ENERGY)}, device_id_type=MESH)
        return carry

    @pl.when(slab > 0)
    def _():
        pl.semaphore_signal(barrier, inc=1, device_id={"slab": slab - 1}, device_id_type=MESH)

    @pl.when(slab < 3)
    def _():
        pl.semaphore_signal(barrier, inc=1, device_id={"slab": slab + 1}, device_id_type=MESH)

    lax.fori_loop(1, ENERGY, greet, 0)

    @pl.when(first)
    def _():
        bef[...] = jnp.zeros_like(bef)

    @pl.when(last)
    def _():
        aft[...] = jnp.zeros_like(aft)

    pl.semaphore_wait(barrier, ENERGY - 1 + jnp.where(slab > 0, 1, 0) + jnp.where(slab < 3, 1, 0))

    def halo(src, k, dst, s_sem, r_sem, to):
        at = pl.ds(k * CHUNK, CHUNK)
        return pltpu.make_async_remote_copy(
            src_ref=src.at[at], dst_ref=dst.at[at], send_sem=s_sem.at[k], recv_sem=r_sem.at[k],
            device_id={"slab": to}, device_id_type=MESH,
        )

    def up(src, k, s_sem, r_sem):
        return halo(src, k, bef, s_sem, r_sem, lax.rem(slab + 1, 4))

    def down(src, k, s_sem, r_sem):
        return halo(src, k, aft, s_sem, r_sem, lax.rem(slab + 3, 4))

    for k in range(4):
        @pl.when(slab < 3)
        def _():
            up(s_h, k, up_s, up_r).start()

        @pl.when(slab > 0)
        def _():
            down(s_h, k, down_s, down_r).start()

    def get(ref, e):
        at = pl.multiple_of(e * 256, 256)
        return ref[pl.ds(at, B), :], ref[pl.ds(at + B, B), :]

    def product(e):
        return term(get(gd, e), get(sig, e)) + term(get(gl, e), get(bef, e)) + term(get(gu, e), get(aft, e))

    def arrived(k, u_r, d_r, u_s, d_s):
        @pl.when(slab > 0)
        def _():
            up(sig, k, u_s, u_r).wait_recv()

        @pl.when(slab < 3)
        def _():
            down(sig, k, d_s, d_r).wait_recv()

    def a_copy(k, peer):
        return pltpu.make_async_remote_copy(
            src_ref=obuf.at[pl.ds(pl.multiple_of(k * CHUNK + peer * 64, 64), 64)],
            dst_ref=recv.at[pl.ds(pl.multiple_of(me * 256 + k * 64, 64), 64)],
            send_sem=a_s.at[0], recv_sem=a_r.at[0],
            device_id={"energy": peer}, device_id_type=MESH,
        )

    def a_own(k):
        return pltpu.make_async_copy(
            obuf.at[pl.ds(pl.multiple_of(k * CHUNK + me * 64, 64), 64)],
            recv.at[pl.ds(pl.multiple_of(me * 256 + k * 64, 64), 64)],
            own_sem.at[k],
        )

    def first_chunk(k, carry):
        for c in loads(k):
            c.wait()
        arrived(k, up_r, down_r, up_s, down_s)

        def some(j, carry):
            for u in range(UNROLL):
                e8 = j * UNROLL + u
                f = product(k * 8 + e8)
                obuf[pl.ds(k * CHUNK + e8, B, stride=16), :] = f[:, :B]
                obuf[pl.ds(k * CHUNK + 8 + e8, B, stride=16), :] = f[:, B:]
            return carry

        lax.fori_loop(0, 8 // UNROLL, some, 0)

        def send(d, carry):
            a_copy(k, lax.rem(me + d, ENERGY)).start()
            return carry

        lax.fori_loop(1, ENERGY, send, 0)
        a_own(k).start()
        return carry

    lax.fori_loop(0, 4, first_chunk, 0)

    @pl.when(slab > 0)
    def _():
        pl.semaphore_signal(credit.at[0], inc=1, device_id={"slab": slab - 1}, device_id_type=MESH)

    @pl.when(slab < 3)
    def _():
        pl.semaphore_signal(credit.at[1], inc=1, device_id={"slab": slab + 1}, device_id_type=MESH)

    fill_tw(tab, tw)
    most = pl.ds(0, 31 * 256)
    sc_copy.wait()
    for k in range(4):
        a_own(k).wait()
    pltpu.make_async_copy(obuf.at[most], obuf.at[most], a_s.at[0]).wait()
    pltpu.make_async_copy(recv.at[most], recv.at[most], a_r.at[0]).wait()

    def b_copy(r, peer):
        return pltpu.make_async_remote_copy(
            src_ref=obuf.at[pl.ds(pl.multiple_of(peer * 256 + r * 64, 64), 64)],
            dst_ref=ret.at[pl.ds(pl.multiple_of(me * 256 + r * 64, 64), 64)],
            send_sem=b_s.at[0], recv_sem=b_r.at[0],
            device_id={"energy": peer}, device_id_type=MESH,
        )

    def b_own(r):
        at = pl.ds(pl.multiple_of(me * 256 + r * 64, 64), 64)
        return pltpu.make_async_copy(obuf.at[at], ret.at[at], own_sem.at[4 + r])

    def convolve_row(r, carry):
        def ld_x(s, c, r0):
            at = s * 256 + (r0 // 8) * 64 + c * 8
            return jnp.concatenate([
                recv[pl.ds(pl.multiple_of(at + r * 16, 8), 8), :],
                recv[pl.ds(pl.multiple_of(at + 64 + r * 16, 8), 8), :],
            ], 0)

        def ld_s(p, c):
            return scr[pl.ds(p * 8 + c * 4 + r, 128, stride=64), :]

        def st_o(d, c, r0, val):
            at = d * 256 + (r0 // 8) * 16 + c * 8
            obuf[pl.ds(pl.multiple_of(at + r * 64, 8), 8), :] = val

        conv_r(ld_x, ld_s, st_o, tw, dm, yh, yl, v)

        def send(d, carry):
            b_copy(r, lax.rem(me + d, ENERGY)).start()
            return carry

        lax.fori_loop(1, ENERGY, send, 0)
        b_own(r).start()
        return carry

    lax.fori_loop(0, 4, convolve_row, 0)
    for r in range(4):
        b_own(r).wait()
    pltpu.make_async_copy(ret.at[most], ret.at[most], b_r.at[0]).wait()

    @pl.when(slab < 3)
    def _():
        pl.semaphore_wait(credit.at[0], 1)

    @pl.when(slab > 0)
    def _():
        pl.semaphore_wait(credit.at[1], 1)

    def renew(k, carry):
        def one(e8, carry):
            mask = kept[...]
            at = pl.multiple_of((k * 8 + e8) * 256, 256)
            for c in range(2):
                rows = pl.ds(at + c * B, B)
                sig[rows, :] = sig[rows, :] + mask * ret[pl.ds(k * 16 + c * 8 + e8, B, stride=64), :]
            return carry

        lax.fori_loop(0, 8, one, 0)

        @pl.when(slab < 3)
        def _():
            up(sig, k, up2_s, up2_r).start()

        @pl.when(slab > 0)
        def _():
            down(sig, k, down2_s, down2_r).start()

        return carry

    lax.fori_loop(0, 4, renew, 0)

    def out_copy(k):
        at = pl.ds(pl.multiple_of(k * CHUNK, CHUNK), CHUNK)
        return pltpu.make_async_copy(recv.at[at], out_h.at[at], out_sem.at[k])

    def second_chunk(k, carry):
        arrived(k, up2_r, down2_r, up2_s, down2_s)

        def some(j, carry):
            for u in range(UNROLL):
                e = k * 8 + j * UNROLL + u
                f = product(e)
                at = pl.multiple_of(e * 256, 256)
                recv[pl.ds(at, B), :] = f[:, :B]
                recv[pl.ds(at + B, B), :] = f[:, B:]
            return carry

        lax.fori_loop(0, 8 // UNROLL, some, 0)
        out_copy(k).start()
        return carry

    lax.fori_loop(0, 4, second_chunk, 0)
    pltpu.make_async_copy(obuf.at[most], obuf.at[most], b_s.at[0]).wait()
    for k in range(4):
        @pl.when(slab < 3)
        def _():
            up(sig, k, up_s, up_r).wait_send()
            up(sig, k, up2_s, up2_r).wait_send()

        @pl.when(slab > 0)
        def _():
            down(sig, k, down_s, down_r).wait_send()
            down(sig, k, down2_s, down2_r).wait_send()

        out_copy(k).wait()


def local(green_diag, green_lower, green_upper, sigma_lesser, screened, pattern):
    fields = [a.reshape(ROWS, B) for a in (green_diag, green_lower, green_upper, sigma_lesser, screened)]
    mask = pattern[0].astype(F32)
    kept = mask[:, None] * mask[None, :]
    hbm = pl.BlockSpec(memory_space=pl.ANY)
    whole = pl.BlockSpec(memory_space=pltpu.VMEM)
    field = pltpu.VMEM((ROWS, B), F32)
    dma = pltpu.SemaphoreType.DMA
    four = dma((4,))
    out = pl.pallas_call(
        kernel,
        out_shape=jax.ShapeDtypeStruct((ROWS, B), F32),
        in_specs=[hbm] * 5 + [whole] * 3,
        out_specs=hbm,
        scratch_shapes=[field] * 10 + [
            pltpu.VMEM((8, 2, B, B), F32), pltpu.VMEM((8, 256, B), BF),
            pltpu.VMEM((8, 256, B), BF), pltpu.VMEM((8, 256, B), F32),
            dma((4, 4)), dma((1,)), dma((8,)), four, four, four, four, four,
            dma((1,)), dma((1,)), dma((1,)), dma((1,)), four, four, four, four,
            pltpu.SemaphoreType.REGULAR((2,)),
        ],
        compiler_params=pltpu.CompilerParams(
            vmem_limit_bytes=63 << 20, collective_id=0, has_side_effects=True
        ),
        name="gw",
    )(*fields, kept, jnp.asarray(dft_mats()), jnp.asarray(tw_tab()))
    return out.reshape(1, 32, 2, B, B)


def solution(mesh):
    return jax.shard_map(
        local,
        mesh=mesh,
        in_specs=(
            P("slab", "energy", None, None, None),
            P("slab", "energy", None, None, None),
            P("slab", "energy", None, None, None),
            P("slab", "energy", None, None, None),
            P("slab", None, None, "energy", None),
            P("slab", None),
        ),
        out_specs=P("slab", "energy", None, None, None),
        check_vma=False,
    )
```

```python
import functools
import math

import jax
import jax.numpy as jnp
import numpy as np
from jax import lax
from jax.experimental import pallas as pl
from jax.experimental.pallas import tpu as pltpu
from jax.sharding import PartitionSpec as P

BF = jnp.bfloat16
F32 = jnp.float32
B = 128
LIMIT = 60 << 20


def split(x):
    h=x.astype(BF); return h,(x-h.astype(F32)).astype(BF)
def rot(h):
    return jnp.concatenate([h, jnp.concatenate([-h[:,128:], h[:,:128]],1)],0)
def dot(a,b): return lax.dot_general(a,b,(((1,),(0,)),((),())),preferred_element_type=F32)
def dott(a,b): return lax.dot_general(a,b,(((1,),(1,)),((),())),preferred_element_type=F32)
def rotT(Tr,Ti):
    return jnp.concatenate([jnp.concatenate([Tr,-Ti],1),jnp.concatenate([Ti,Tr],1)],0)
def term(G,S):
    Gh,Gl=split(jnp.concatenate([G[0],G[1]],1)); Sh,Sl=split(jnp.concatenate([S[0],S[1]],1))
    tr,ti=G[0].T,G[1].T
    trh,trl=split(tr); tih,til=split(ti)
    Wh=rotT(trh,tih); Wl=rotT(trl,til)
    T2=dot(jnp.concatenate([Gh,Gl],0),rot(Sh)); T=T2[:128]+T2[128:]+dot(Gh,rot(Sl))
    Th,Tl=split(T)
    F2=dot(jnp.concatenate([Th,Tl],0),Wh)
    return F2[:128]+F2[128:]+dot(Th,Wl)

def dft_mats():
    a=np.arange(128); th=2*np.pi*((a[:,None]*a[None,:])%128)/128
    C,S=np.cos(th),np.sin(th)
    f=np.block([[C,S],[-S,C]]); b=np.block([[C,-S],[S,C]])
    out=[]
    for m in (f,b):
        h=m.astype(np.float32).astype(BF); l=(m-h.astype(np.float64)).astype(np.float32).astype(BF)
        out.append(np.concatenate([h,l],0))
    return np.stack(out)
def tw_tab():
    a=np.arange(128)[:,None]; p=np.arange(8)[None,:]
    th=2*np.pi*(a*p)/1024
    t=np.zeros((128,128),np.float32); t[:,:8]=np.cos(th); t[:,8:16]=np.sin(th)
    return t

R2=math.sqrt(0.5)
def radix8(x,sign):
    add=lambda u,v:(u[0]+v[0],u[1]+v[1]); sub=lambda u,v:(u[0]-v[0],u[1]-v[1])
    mi=(lambda u:(u[1],-u[0])) if sign<0 else (lambda u:(-u[1],u[0]))
    def r4(y):
        s0,d0=add(y[0],y[2]),sub(y[0],y[2]); s1,d1=add(y[1],y[3]),mi(sub(y[1],y[3]))
        return [add(s0,s1),add(d0,d1),sub(s0,s1),sub(d0,d1)]
    e=r4(x[0::2]); o=r4(x[1::2])
    def w1(u):
        m=mi(u); return ((u[0]+m[0])*R2,(u[1]+m[1])*R2)
    o=[o[0],w1(o[1]),mi(o[2]),w1(mi(o[3]))]
    return [add(e[k],o[k]) for k in range(4)]+[sub(e[k],o[k]) for k in range(4)]
def conv_r(ld_x,ld_s,st_o,scale,tw,dm,yh,yl,v):
    for ch in range(8):
        x=[(ld_x(4*b+ch//2,0,(ch%2)*16),ld_x(4*b+ch//2,1,(ch%2)*16)) for b in range(8)]
        y=radix8(x,-1)
        rs=slice(ch*16,ch*16+16)
        for p in range(8):
            re,im=y[p]
            if p:
                c,s=tw[p,0,rs,:],tw[p,1,rs,:]
                re,im=re*c+im*s,im*c-re*s
            for k,val in enumerate((re,im)):
                h,l=split(val)
                yh[p,k*128+ch*16:k*128+ch*16+16,:]=h; yl[p,k*128+ch*16:k*128+ch*16+16,:]=l
    for pp in range(4):
        p0,p1=2*pp,2*pp+1
        H=jnp.concatenate([yh[p0],yh[p1]],1); L=jnp.concatenate([yl[p0],yl[p1]],1)
        D=dm[0]
        A=dot(D,H); Z=A[:256]+A[256:]+dot(D[:256],L)
        wr=jnp.concatenate([ld_s(p0,0),ld_s(p1,0)],1); wi=jnp.concatenate([ld_s(p0,1),ld_s(p1,1)],1)
        zr,zi=Z[:128],Z[128:]
        Q=jnp.concatenate([zr*wr-zi*wi,zr*wi+zi*wr],0)
        h,l=split(Q)
        D=dm[1]
        A=dot(D,h); V=A[:256]+A[256:]+dot(D[:256],l)
        v[p0]=V[:,:128]; v[p1]=V[:,128:]
    for ch in range(16):
        rs=slice(ch*8,ch*8+8); ri=slice(128+ch*8,128+ch*8+8)
        x=[]
        for p in range(8):
            re,im=v[p,rs,:],v[p,ri,:]
            if p:
                c,s=tw[p,0,rs,:],tw[p,1,rs,:]
                re,im=re*c-im*s,im*c+re*s
            x.append((re,im))
        y=radix8(x,1)
        for b in range(8):
            d=4*b+ch//4
            st_o(d,0,(ch%4)*8,y[b][1]*(-scale)); st_o(d,1,(ch%4)*8,y[b][0]*scale)
def fill_tw(tab,tw):
    for p in range(1,8):
        tw[p,0]=jnp.broadcast_to(tab[:,p:p+1],(128,128)); tw[p,1]=jnp.broadcast_to(tab[:,8+p:9+p],(128,128))

ENERGY = 32
ROWS = 8192
CHUNK = 2048
UNROLL = 4
MESH = pl.DeviceIdType.MESH


def kernel(
    gd_h, gl_h, gu_h, s_h, sc_h, pat, row_on, dm, tab, out_h,
    gd, gn, gx, sig, near, cross, obuf, recv, ret, rx, scr, tw, yh, yl, v,
    load_sem, sc_sem, own_sem, out_sem, n_s, n_r, x_s, x_r,
    a_s, a_r, b_s, b_r, c_s, c_r, n2_s, n2_r, credit,
):
    me = lax.axis_index("energy")
    slab = lax.axis_index("slab")
    odd = lax.rem(slab, 2)
    has_cross = jnp.logical_or(slab == 1, slab == 2)
    near_slab = slab + 1 - 2 * odd
    cross_slab = 3 - slab

    def load(k, j, src, dst):
        at = pl.ds(pl.multiple_of(k * CHUNK, CHUNK), CHUNK)
        return pltpu.make_async_copy(src.at[at], dst.at[at], load_sem.at[j, k])

    sc_copy = pltpu.make_async_copy(sc_h, scr, sc_sem.at[0])
    for k in range(4):
        load(k, 0, s_h, sig).start()
        load(k, 1, gd_h, gd).start()

        @pl.when(odd == 0)
        def _():
            load(k, 2, gu_h, gn).start()
            load(k, 3, gl_h, gx).start()

        @pl.when(odd == 1)
        def _():
            load(k, 2, gl_h, gn).start()
            load(k, 3, gu_h, gx).start()

    sc_copy.start()

    barrier = pltpu.get_barrier_semaphore()
    pl.semaphore_signal(barrier, inc=1, device_id={"slab": near_slab}, device_id_type=MESH)

    @pl.when(has_cross)
    def _():
        def greet_cross(d, carry):
            pl.semaphore_signal(
                barrier, inc=1,
                device_id={"energy": lax.rem(me + d, ENERGY), "slab": cross_slab}, device_id_type=MESH,
            )
            return carry

        lax.fori_loop(0, ENERGY, greet_cross, 0)

    def greet(d, carry):
        pl.semaphore_signal(barrier, inc=1, device_id={"energy": lax.rem(me + d, ENERGY)}, device_id_type=MESH)
        return carry

    lax.fori_loop(1, ENERGY, greet, 0)

    @pl.when(jnp.logical_not(has_cross))
    def _():
        cross[...] = jnp.zeros_like(cross)

    fill_tw(tab, tw)
    pl.semaphore_wait(barrier, ENERGY + jnp.where(has_cross, ENERGY, 0))

    def halo(src, k, dst, s_sem, r_sem, to):
        at = pl.ds(pl.multiple_of(k * CHUNK, CHUNK), CHUNK)
        return pltpu.make_async_remote_copy(
            src_ref=src.at[at], dst_ref=dst.at[at], send_sem=s_sem.at[k], recv_sem=r_sem.at[k],
            device_id={"slab": to}, device_id_type=MESH,
        )

    def to_near(k):
        return halo(s_h, k, near, n_s, n_r, near_slab)

    def to_cross(k):
        return halo(s_h, k, cross, x_s, x_r, cross_slab)

    def to_near_again(k):
        return halo(sig, k, near, n2_s, n2_r, near_slab)

    for k in range(4):
        @pl.when(has_cross)
        def _():
            to_cross(k).start()

        to_near(k).start()

    def get(ref, e):
        at = pl.multiple_of(e * 256, 256)
        return ref[pl.ds(at, B), :], ref[pl.ds(at + B, B), :]

    def own_near(e):
        return term(get(gd, e), get(sig, e)) + term(get(gn, e), get(near, e))

    def each(k, body):
        def some(j, carry):
            for u in range(UNROLL):
                body(j * UNROLL + u, k * 8 + j * UNROLL + u)
            return carry

        lax.fori_loop(0, 8 // UNROLL, some, 0)

    def a_copy(k, peer):
        return pltpu.make_async_remote_copy(
            src_ref=obuf.at[pl.ds(pl.multiple_of(k * CHUNK + peer * 64, 64), 64)],
            dst_ref=recv.at[pl.ds(pl.multiple_of(me * 256 + k * 64, 64), 64)],
            send_sem=a_s.at[0], recv_sem=a_r.at[0],
            device_id={"energy": peer}, device_id_type=MESH,
        )

    def a_own(k):
        return pltpu.make_async_copy(
            obuf.at[pl.ds(pl.multiple_of(k * CHUNK + me * 64, 64), 64)],
            recv.at[pl.ds(pl.multiple_of(me * 256 + k * 64, 64), 64)],
            own_sem.at[k],
        )

    def put(ref, e, f):
        at = pl.multiple_of(e * 256, 256)
        ref[pl.ds(at, B), :] = f[:, :B]
        ref[pl.ds(at + B, B), :] = f[:, B:]

    def first_part(k, carry):
        load(k, 0, s_h, sig).wait()
        load(k, 1, gd_h, gd).wait()
        load(k, 2, gu_h, gn).wait()
        to_near(k).wait_recv()
        each(k, lambda e8, e: put(ret, e, own_near(e)))
        return carry

    lax.fori_loop(0, 4, first_part, 0)
    pl.semaphore_signal(credit.at[0], inc=1, device_id={"slab": near_slab}, device_id_type=MESH)

    def first_cross(k, carry):
        load(k, 3, gl_h, gx).wait()

        @pl.when(has_cross)
        def _():
            to_cross(k).wait_recv()

        def add(e8, e):
            f = term(get(gx, e), get(cross, e))
            re, im = get(ret, e)
            obuf[pl.ds(k * CHUNK + e8, B, stride=16), :] = re + f[:, :B]
            obuf[pl.ds(k * CHUNK + 8 + e8, B, stride=16), :] = im + f[:, B:]

        each(k, add)

        def send(d, carry):
            a_copy(k, lax.rem(me + d, ENERGY)).start()
            return carry

        lax.fori_loop(1, ENERGY, send, 0)
        a_own(k).start()
        return carry

    lax.fori_loop(0, 4, first_cross, 0)

    most = pl.ds(0, 31 * 256)
    sc_copy.wait()
    for k in range(4):
        a_own(k).wait()
    pltpu.make_async_copy(obuf.at[most], obuf.at[most], a_s.at[0]).wait()
    pltpu.make_async_copy(recv.at[most], recv.at[most], a_r.at[0]).wait()

    def b_copy(k, peer, off, size):
        return pltpu.make_async_remote_copy(
            src_ref=obuf.at[pl.ds(pl.multiple_of(k * CHUNK + peer * 64 + off, 16), size)],
            dst_ref=ret.at[pl.ds(pl.multiple_of(k * CHUNK + me * 64 + off, 16), size)],
            send_sem=b_s.at[0], recv_sem=b_r.at[k],
            device_id={"energy": peer}, device_id_type=MESH,
        )

    def c_copy(k, peer, off, size):
        return pltpu.make_async_remote_copy(
            src_ref=obuf.at[pl.ds(pl.multiple_of(k * CHUNK + peer * 64 + off, 16), size)],
            dst_ref=rx.at[pl.ds(pl.multiple_of(k * CHUNK + me * 64 + off, 16), size)],
            send_sem=c_s.at[0], recv_sem=c_r.at[k],
            device_id={"energy": peer, "slab": cross_slab}, device_id_type=MESH,
        )

    def b_own(k):
        at = pl.ds(pl.multiple_of(k * CHUNK + me * 64, 64), 64)
        return pltpu.make_async_copy(obuf.at[at], ret.at[at], own_sem.at[4 + k])

    def scatter(k, off, size):
        @pl.when(has_cross)
        def _():
            def both(d, carry):
                peer = lax.rem(me + d, ENERGY)
                b_copy(k, peer, off, size).start()
                c_copy(k, peer, off, size).start()
                return carry

            lax.fori_loop(1, ENERGY, both, 0)
            c_copy(k, me, off, size).start()

        @pl.when(jnp.logical_not(has_cross))
        def _():
            def one(d, carry):
                b_copy(k, lax.rem(me + d, ENERGY), off, size).start()
                return carry

            lax.fori_loop(1, ENERGY, one, 0)

    columns = pat[...].astype(F32)

    def convolve_row(r, carry):
        def ld_x(s, c, r0):
            at = s * 256 + (r0 // 8) * 64 + c * 8
            return jnp.concatenate([
                recv[pl.ds(pl.multiple_of(at + r * 16, 8), 8), :],
                recv[pl.ds(pl.multiple_of(at + 64 + r * 16, 8), 8), :],
            ], 0)

        def ld_s(p, c):
            return scr[pl.ds(p * 8 + c * 4 + r, 128, stride=64), :]

        def st_o(d, c, r0, val):
            at = (r0 // 8) * CHUNK + d * 64 + c * 8
            obuf[pl.ds(pl.multiple_of(at + r * 16, 8), 8), :] = val

        scale = columns * (row_on[0, me * 4 + r].astype(F32) * (1.0 / 1024))
        conv_r(ld_x, ld_s, st_o, scale, tw, dm, yh, yl, v)
        scatter(0, r * 16, 16)
        return carry

    lax.fori_loop(0, 4, convolve_row, 0)
    for k in range(1, 4):
        scatter(k, 0, 64)
    for k in range(4):
        b_own(k).start()
    pl.semaphore_wait(credit.at[0], 1)

    def out_copy(k):
        at = pl.ds(pl.multiple_of(k * CHUNK, CHUNK), CHUNK)
        return pltpu.make_async_copy(recv.at[at], out_h.at[at], out_sem.at[k])

    def update(field, new, k):
        def one(e8, carry):
            at = pl.multiple_of((k * 8 + e8) * 256, 256)
            for c in range(2):
                rows = pl.ds(at + c * B, B)
                field[rows, :] = field[rows, :] + new[pl.ds(k * CHUNK + c * 8 + e8, B, stride=16), :]
            return carry

        lax.fori_loop(0, 8, one, 0)

    def second_chunk(k, carry):
        at = pl.multiple_of(k * CHUNK, CHUNK)
        part = pl.ds(at, 31 * 64)
        b_own(k).wait()
        pltpu.make_async_copy(ret.at[part], ret.at[part], b_r.at[k]).wait()
        update(sig, ret, k)
        to_near_again(k).start()

        @pl.when(has_cross)
        def _():
            part = pl.ds(at, CHUNK)
            pltpu.make_async_copy(rx.at[part], rx.at[part], c_r.at[k]).wait()
            update(cross, rx, k)

        def own_cross(e8, e):
            put(recv, e, term(get(gd, e), get(sig, e)) + term(get(gx, e), get(cross, e)))

        each(k, own_cross)
        to_near_again(k).wait_recv()

        def add(e8, e):
            f = term(get(gn, e), get(near, e))
            re, im = get(recv, e)
            put(recv, e, jnp.concatenate([re, im], 1) + f)

        each(k, add)
        out_copy(k).start()
        return carry

    lax.fori_loop(0, 4, second_chunk, 0)
    pltpu.make_async_copy(obuf.at[most], obuf.at[most], b_s.at[0]).wait()

    @pl.when(has_cross)
    def _():
        pltpu.make_async_copy(obuf, obuf, c_s.at[0]).wait()
        for k in range(4):
            to_cross(k).wait_send()

    for k in range(4):
        to_near(k).wait_send()
        to_near_again(k).wait_send()
        out_copy(k).wait()


def local(green_diag, green_lower, green_upper, sigma_lesser, screened, pattern):
    fields = [a.reshape(ROWS, B) for a in (green_diag, green_lower, green_upper, sigma_lesser, screened)]
    hbm = pl.BlockSpec(memory_space=pl.ANY)
    whole = pl.BlockSpec(memory_space=pltpu.VMEM)
    field = pltpu.VMEM((ROWS, B), F32)
    dma = pltpu.SemaphoreType.DMA
    one, four = dma((1,)), dma((4,))
    out = pl.pallas_call(
        kernel,
        out_shape=jax.ShapeDtypeStruct((ROWS, B), F32),
        in_specs=[hbm] * 5 + [whole, pl.BlockSpec(memory_space=pltpu.SMEM), whole, whole],
        out_specs=hbm,
        scratch_shapes=[field] * 11 + [
            pltpu.VMEM((8, 2, B, B), F32), pltpu.VMEM((8, 256, B), BF),
            pltpu.VMEM((8, 256, B), BF), pltpu.VMEM((8, 256, B), F32),
            dma((4, 4)), one, dma((8,)), four, four, four, four, four,
            one, one, one, four, one, four, four, four,
            pltpu.SemaphoreType.REGULAR((1,)),
        ],
        compiler_params=pltpu.CompilerParams(
            vmem_limit_bytes=63 << 20, collective_id=0, has_side_effects=True
        ),
        name="gw",
    )(*fields, pattern, pattern, jnp.asarray(dft_mats()), jnp.asarray(tw_tab()))
    return out.reshape(1, 32, 2, B, B)


def solution(mesh):
    return jax.shard_map(
        local,
        mesh=mesh,
        in_specs=(
            P("slab", "energy", None, None, None),
            P("slab", "energy", None, None, None),
            P("slab", "energy", None, None, None),
            P("slab", "energy", None, None, None),
            P("slab", None, None, "energy", None),
            P("slab", None),
        ),
        out_specs=P("slab", "energy", None, None, None),
        check_vma=False,
    )
```

```python
import functools
import math

import jax
import jax.numpy as jnp
import numpy as np
from jax import lax
from jax.experimental import pallas as pl
from jax.experimental.pallas import tpu as pltpu
from jax.sharding import PartitionSpec as P

BF = jnp.bfloat16
F32 = jnp.float32
B = 128
LIMIT = 60 << 20


def split(x):
    h=x.astype(BF); return h,(x-h.astype(F32)).astype(BF)
def rot(h):
    return jnp.concatenate([h, jnp.concatenate([-h[:,128:], h[:,:128]],1)],0)
def dot(a,b): return lax.dot_general(a,b,(((1,),(0,)),((),())),preferred_element_type=F32)
def dott(a,b): return lax.dot_general(a,b,(((1,),(1,)),((),())),preferred_element_type=F32)
def rotT(Tr,Ti):
    return jnp.concatenate([jnp.concatenate([Tr,-Ti],1),jnp.concatenate([Ti,Tr],1)],0)
def term(G,S):
    Gh,Gl=split(jnp.concatenate([G[0],G[1]],1)); Sh,Sl=split(jnp.concatenate([S[0],S[1]],1))
    tr,ti=G[0].T,G[1].T
    trh,trl=split(tr); tih,til=split(ti)
    Wh=rotT(trh,tih); Wl=rotT(trl,til)
    T2=dot(jnp.concatenate([Gh,Gl],0),rot(Sh)); T=T2[:128]+T2[128:]+dot(Gh,rot(Sl))
    Th,Tl=split(T)
    F2=dot(jnp.concatenate([Th,Tl],0),Wh)
    return F2[:128]+F2[128:]+dot(Th,Wl)

def dft_mats():
    a=np.arange(128); th=2*np.pi*((a[:,None]*a[None,:])%128)/128
    C,S=np.cos(th),np.sin(th)
    f=np.block([[C,S],[-S,C]]); b=np.block([[C,-S],[S,C]])
    out=[]
    for m in (f,b):
        h=m.astype(np.float32).astype(BF); l=(m-h.astype(np.float64)).astype(np.float32).astype(BF)
        out.append(np.concatenate([h,l],0))
    return np.stack(out)
def tw_tab():
    a=np.arange(128)[:,None]; p=np.arange(8)[None,:]
    th=2*np.pi*(a*p)/1024
    t=np.zeros((128,128),np.float32); t[:,:8]=np.cos(th); t[:,8:16]=np.sin(th)
    return t

R2=math.sqrt(0.5)
def radix8(x,sign):
    add=lambda u,v:(u[0]+v[0],u[1]+v[1]); sub=lambda u,v:(u[0]-v[0],u[1]-v[1])
    mi=(lambda u:(u[1],-u[0])) if sign<0 else (lambda u:(-u[1],u[0]))
    def r4(y):
        s0,d0=add(y[0],y[2]),sub(y[0],y[2]); s1,d1=add(y[1],y[3]),mi(sub(y[1],y[3]))
        return [add(s0,s1),add(d0,d1),sub(s0,s1),sub(d0,d1)]
    e=r4(x[0::2]); o=r4(x[1::2])
    def w1(u):
        m=mi(u); return ((u[0]+m[0])*R2,(u[1]+m[1])*R2)
    o=[o[0],w1(o[1]),mi(o[2]),w1(mi(o[3]))]
    return [add(e[k],o[k]) for k in range(4)]+[sub(e[k],o[k]) for k in range(4)]
def conv_r(ld_x,ld_s,st_o,scale,tw,dm,yh,yl,v):
    for ch in range(8):
        x=[(ld_x(4*b+ch//2,0,(ch%2)*16),ld_x(4*b+ch//2,1,(ch%2)*16)) for b in range(8)]
        y=radix8(x,-1)
        rs=slice(ch*16,ch*16+16)
        for p in range(8):
            re,im=y[p]
            if p:
                c,s=tw[p,0,rs,:],tw[p,1,rs,:]
                re,im=re*c+im*s,im*c-re*s
            for k,val in enumerate((re,im)):
                h,l=split(val)
                yh[p,k*128+ch*16:k*128+ch*16+16,:]=h; yl[p,k*128+ch*16:k*128+ch*16+16,:]=l
    for pp in range(4):
        p0,p1=2*pp,2*pp+1
        H=jnp.concatenate([yh[p0],yh[p1]],1); L=jnp.concatenate([yl[p0],yl[p1]],1)
        D=dm[0]
        A=dot(D,H); Z=A[:256]+A[256:]+dot(D[:256],L)
        wr=jnp.concatenate([ld_s(p0,0),ld_s(p1,0)],1); wi=jnp.concatenate([ld_s(p0,1),ld_s(p1,1)],1)
        zr,zi=Z[:128],Z[128:]
        Q=jnp.concatenate([zr*wr-zi*wi,zr*wi+zi*wr],0)
        h,l=split(Q)
        D=dm[1]
        A=dot(D,h); V=A[:256]+A[256:]+dot(D[:256],l)
        v[p0]=V[:,:128]; v[p1]=V[:,128:]
    for ch in range(16):
        rs=slice(ch*8,ch*8+8); ri=slice(128+ch*8,128+ch*8+8)
        x=[]
        for p in range(8):
            re,im=v[p,rs,:],v[p,ri,:]
            if p:
                c,s=tw[p,0,rs,:],tw[p,1,rs,:]
                re,im=re*c-im*s,im*c+re*s
            x.append((re,im))
        y=radix8(x,1)
        for b in range(8):
            d=4*b+ch//4
            st_o(d,0,(ch%4)*8,y[b][1]*(-scale)); st_o(d,1,(ch%4)*8,y[b][0]*scale)
def fill_tw(tab,tw):
    for p in range(1,8):
        tw[p,0]=jnp.broadcast_to(tab[:,p:p+1],(128,128)); tw[p,1]=jnp.broadcast_to(tab[:,8+p:9+p],(128,128))

ENERGY = 32
ROWS = 8192
CHUNK = 2048
UNROLL = 4
MESH = pl.DeviceIdType.MESH


def kernel(
    gd_h, gl_h, gu_h, s_h, sc_h, pat, row_on, dm_h, tab_h, out,
    gd, gn, gx, sig, near, cross, obuf, recv, ret, rx, scr, tw, yh, yl, v, dm, tab,
    load_sem, sc_sem, own_sem, n_s, n_r, x_s, x_r,
    a_s, a_r, b_s, b_r, c_s, c_r, n2_s, n2_r, credit,
):
    me = lax.axis_index("energy")
    slab = lax.axis_index("slab")
    odd = lax.rem(slab, 2)
    has_cross = jnp.logical_or(slab == 1, slab == 2)
    near_slab = slab + 1 - 2 * odd
    cross_slab = 3 - slab

    def load(k, j, src, dst):
        at = pl.ds(pl.multiple_of(k * CHUNK, CHUNK), CHUNK)
        return pltpu.make_async_copy(src.at[at], dst.at[at], load_sem.at[j, k])

    sc_copy = pltpu.make_async_copy(sc_h, scr, sc_sem.at[0])
    for k in range(4):
        load(k, 0, s_h, sig).start()
        load(k, 1, gd_h, gd).start()

        @pl.when(odd == 0)
        def _():
            load(k, 2, gu_h, gn).start()
            load(k, 3, gl_h, gx).start()

        @pl.when(odd == 1)
        def _():
            load(k, 2, gl_h, gn).start()
            load(k, 3, gu_h, gx).start()

    sc_copy.start()
    tab_copy = pltpu.make_async_copy(tab_h, tab, sc_sem.at[1])
    dm_copy = pltpu.make_async_copy(dm_h, dm, sc_sem.at[2])
    tab_copy.start()
    dm_copy.start()

    barrier = pltpu.get_barrier_semaphore()
    pl.semaphore_signal(barrier, inc=1, device_id={"slab": near_slab}, device_id_type=MESH)

    @pl.when(has_cross)
    def _():
        def greet_cross(d, carry):
            pl.semaphore_signal(
                barrier, inc=1,
                device_id={"energy": lax.rem(me + d, ENERGY), "slab": cross_slab}, device_id_type=MESH,
            )
            return carry

        lax.fori_loop(0, ENERGY, greet_cross, 0)

    def greet(d, carry):
        pl.semaphore_signal(barrier, inc=1, device_id={"energy": lax.rem(me + d, ENERGY)}, device_id_type=MESH)
        return carry

    lax.fori_loop(1, ENERGY, greet, 0)

    @pl.when(jnp.logical_not(has_cross))
    def _():
        cross[...] = jnp.zeros_like(cross)
        rx[...] = jnp.zeros_like(rx)

    tab_copy.wait()
    fill_tw(tab, tw)
    pl.semaphore_wait(barrier, ENERGY + jnp.where(has_cross, ENERGY, 0))

    def halo(src, k, dst, s_sem, r_sem, to):
        at = pl.ds(pl.multiple_of(k * CHUNK, CHUNK), CHUNK)
        return pltpu.make_async_remote_copy(
            src_ref=src.at[at], dst_ref=dst.at[at], send_sem=s_sem.at[k], recv_sem=r_sem.at[k],
            device_id={"slab": to}, device_id_type=MESH,
        )

    def to_near(k):
        return halo(s_h, k, near, n_s, n_r, near_slab)

    def to_cross(k):
        return halo(s_h, k, cross, x_s, x_r, cross_slab)

    def to_near_again(k):
        return halo(sig, k, near, n2_s, n2_r, near_slab)

    for k in range(4):
        @pl.when(has_cross)
        def _():
            to_cross(k).start()

        to_near(k).start()

    def get(ref, e):
        at = pl.multiple_of(e * 256, 256)
        return ref[pl.ds(at, B), :], ref[pl.ds(at + B, B), :]

    def own_near(e):
        return term(get(gd, e), get(sig, e)) + term(get(gn, e), get(near, e))

    def each(k, body):
        def some(j, carry):
            for u in range(UNROLL):
                body(j * UNROLL + u, k * 8 + j * UNROLL + u)
            return carry

        lax.fori_loop(0, 8 // UNROLL, some, 0)

    def a_copy(k, peer):
        return pltpu.make_async_remote_copy(
            src_ref=obuf.at[pl.ds(pl.multiple_of(k * CHUNK + peer * 64, 64), 64)],
            dst_ref=recv.at[pl.ds(pl.multiple_of(me * 256 + k * 64, 64), 64)],
            send_sem=a_s.at[0], recv_sem=a_r.at[0],
            device_id={"energy": peer}, device_id_type=MESH,
        )

    def a_own(k):
        return pltpu.make_async_copy(
            obuf.at[pl.ds(pl.multiple_of(k * CHUNK + me * 64, 64), 64)],
            recv.at[pl.ds(pl.multiple_of(me * 256 + k * 64, 64), 64)],
            own_sem.at[k],
        )

    def put(ref, e, f):
        at = pl.multiple_of(e * 256, 256)
        ref[pl.ds(at, B), :] = f[:, :B]
        ref[pl.ds(at + B, B), :] = f[:, B:]

    def first_part(k, carry):
        load(k, 0, s_h, sig).wait()
        load(k, 1, gd_h, gd).wait()
        load(k, 2, gu_h, gn).wait()
        to_near(k).wait_recv()
        each(k, lambda e8, e: put(ret, e, own_near(e)))
        return carry

    lax.fori_loop(0, 4, first_part, 0)
    pl.semaphore_signal(credit.at[0], inc=1, device_id={"slab": near_slab}, device_id_type=MESH)

    def first_cross(k, carry):
        load(k, 3, gl_h, gx).wait()

        @pl.when(has_cross)
        def _():
            to_cross(k).wait_recv()

        def add(e8, e):
            f = term(get(gx, e), get(cross, e))
            re, im = get(ret, e)
            obuf[pl.ds(k * CHUNK + e8, B, stride=16), :] = re + f[:, :B]
            obuf[pl.ds(k * CHUNK + 8 + e8, B, stride=16), :] = im + f[:, B:]

        each(k, add)

        def send(d, carry):
            a_copy(k, lax.rem(me + d, ENERGY)).start()
            return carry

        lax.fori_loop(1, ENERGY, send, 0)
        a_own(k).start()
        return carry

    lax.fori_loop(0, 4, first_cross, 0)

    most = pl.ds(0, 31 * 256)
    sc_copy.wait()
    dm_copy.wait()
    for k in range(4):
        a_own(k).wait()
    pltpu.make_async_copy(obuf.at[most], obuf.at[most], a_s.at[0]).wait()
    pltpu.make_async_copy(recv.at[most], recv.at[most], a_r.at[0]).wait()

    def b_copy(k, peer, off, size):
        return pltpu.make_async_remote_copy(
            src_ref=obuf.at[pl.ds(pl.multiple_of(k * CHUNK + peer * 64 + off, 16), size)],
            dst_ref=ret.at[pl.ds(pl.multiple_of(k * CHUNK + me * 64 + off, 16), size)],
            send_sem=b_s.at[0], recv_sem=b_r.at[k],
            device_id={"energy": peer}, device_id_type=MESH,
        )

    def c_copy(k, peer, off, size):
        return pltpu.make_async_remote_copy(
            src_ref=obuf.at[pl.ds(pl.multiple_of(k * CHUNK + peer * 64 + off, 16), size)],
            dst_ref=rx.at[pl.ds(pl.multiple_of(k * CHUNK + me * 64 + off, 16), size)],
            send_sem=c_s.at[0], recv_sem=c_r.at[k],
            device_id={"energy": peer, "slab": cross_slab}, device_id_type=MESH,
        )

    def b_own(k):
        at = pl.ds(pl.multiple_of(k * CHUNK + me * 64, 64), 64)
        return pltpu.make_async_copy(obuf.at[at], ret.at[at], own_sem.at[4 + k])

    def scatter_both(k, off, size):
        def both(d, carry):
            peer = lax.rem(me + d, ENERGY)
            b_copy(k, peer, off, size).start()
            c_copy(k, peer, off, size).start()
            return carry

        lax.fori_loop(1, ENERGY, both, 0)
        c_copy(k, me, off, size).start()

    def scatter_own(k):
        def one(d, carry):
            b_copy(k, lax.rem(me + d, ENERGY), 0, 64).start()
            return carry

        lax.fori_loop(1, ENERGY, one, 0)

    @pl.when(has_cross)
    def _():
        pl.semaphore_signal(credit.at[1], inc=1, device_id={"slab": near_slab}, device_id_type=MESH)

    columns = pat[...].astype(F32)

    def convolve_row(r, carry):
        def ld_x(s, c, r0):
            at = s * 256 + (r0 // 8) * 64 + c * 8
            return jnp.concatenate([
                recv[pl.ds(pl.multiple_of(at + r * 16, 8), 8), :],
                recv[pl.ds(pl.multiple_of(at + 64 + r * 16, 8), 8), :],
            ], 0)

        def ld_s(p, c):
            return scr[pl.ds(p * 8 + c * 4 + r, 128, stride=64), :]

        def st_o(d, c, r0, val):
            at = (r0 // 8) * CHUNK + d * 64 + c * 8
            obuf[pl.ds(pl.multiple_of(at + r * 16, 8), 8), :] = val

        scale = columns * (row_on[0, me * 4 + r].astype(F32) * (1.0 / 1024))
        conv_r(ld_x, ld_s, st_o, scale, tw, dm, yh, yl, v)

        @pl.when(has_cross)
        def _():
            scatter_both(0, r * 16, 16)

        return carry

    lax.fori_loop(0, 4, convolve_row, 0)

    @pl.when(has_cross)
    def _():
        for k in range(1, 4):
            scatter_both(k, 0, 64)

    @pl.when(jnp.logical_not(has_cross))
    def _():
        pl.semaphore_wait(credit.at[1], 1)
        for k in range(4):
            scatter_own(k)

    for k in range(4):
        b_own(k).start()
    pl.semaphore_wait(credit.at[0], 1)

    def update(field, new, k):
        def one(e8, carry):
            at = pl.multiple_of((k * 8 + e8) * 256, 256)
            for c in range(2):
                rows = pl.ds(at + c * B, B)
                field[rows, :] = field[rows, :] + new[pl.ds(k * CHUNK + c * 8 + e8, B, stride=16), :]
            return carry

        lax.fori_loop(0, 8, one, 0)

    def second_chunk(k, carry):
        at = pl.multiple_of(k * CHUNK, CHUNK)
        part = pl.ds(at, 31 * 64)
        b_own(k).wait()
        pltpu.make_async_copy(ret.at[part], ret.at[part], b_r.at[k]).wait()
        update(sig, ret, k)
        to_near_again(k).start()

        @pl.when(has_cross)
        def _():
            part = pl.ds(at, CHUNK)
            pltpu.make_async_copy(rx.at[part], rx.at[part], c_r.at[k]).wait()

        def own_cross(e8, e):
            re, im = get(cross, e)
            new = [rx[pl.ds(k * CHUNK + c * 8 + e8, B, stride=16), :] for c in range(2)]
            put(recv, e, term(get(gd, e), get(sig, e)) + term(get(gx, e), (re + new[0], im + new[1])))

        each(k, own_cross)
        to_near_again(k).wait_recv()

        def add(e8, e):
            f = term(get(gn, e), get(near, e))
            re, im = get(recv, e)
            put(out, e, jnp.concatenate([re, im], 1) + f)

        each(k, add)
        return carry

    lax.fori_loop(0, 4, second_chunk, 0)
    pltpu.make_async_copy(obuf.at[most], obuf.at[most], b_s.at[0]).wait()

    @pl.when(has_cross)
    def _():
        pltpu.make_async_copy(obuf, obuf, c_s.at[0]).wait()
        for k in range(4):
            to_cross(k).wait_send()

    for k in range(4):
        to_near(k).wait_send()
        to_near_again(k).wait_send()


def local(green_diag, green_lower, green_upper, sigma_lesser, screened, pattern):
    fields = [a.reshape(ROWS, B) for a in (green_diag, green_lower, green_upper, sigma_lesser, screened)]
    hbm = pl.BlockSpec(memory_space=pl.ANY)
    whole = pl.BlockSpec(memory_space=pltpu.VMEM)
    field = pltpu.VMEM((ROWS, B), F32)
    dma = pltpu.SemaphoreType.DMA
    one, four = dma((1,)), dma((4,))
    out = pl.pallas_call(
        kernel,
        out_shape=pltpu.VMEM((ROWS, B), F32),
        in_specs=[hbm] * 5 + [whole, pl.BlockSpec(memory_space=pltpu.SMEM), hbm, hbm],
        out_specs=whole,
        scratch_shapes=[field] * 11 + [
            pltpu.VMEM((8, 2, B, B), F32), pltpu.VMEM((8, 256, B), BF),
            pltpu.VMEM((8, 256, B), BF), pltpu.VMEM((8, 256, B), F32),
            pltpu.VMEM((2, 512, 256), BF), pltpu.VMEM((B, B), F32),
            dma((4, 4)), dma((3,)), dma((8,)), four, four, four, four,
            one, one, one, four, one, four, four, four,
            pltpu.SemaphoreType.REGULAR((2,)),
        ],
        compiler_params=pltpu.CompilerParams(
            vmem_limit_bytes=55 << 20, collective_id=0, has_side_effects=True
        ),
        name="gw",
    )(*fields, pattern, pattern, jnp.asarray(dft_mats()), jnp.asarray(tw_tab()))
    return out.reshape(1, 32, 2, B, B)


def solution(mesh):
    return jax.shard_map(
        local,
        mesh=mesh,
        in_specs=(
            P("slab", "energy", None, None, None),
            P("slab", "energy", None, None, None),
            P("slab", "energy", None, None, None),
            P("slab", "energy", None, None, None),
            P("slab", None, None, "energy", None),
            P("slab", None),
        ),
        out_specs=P("slab", "energy", None, None, None),
        check_vma=False,
    )
```

```python
import functools
import math

import jax
import jax.numpy as jnp
import numpy as np
from jax import lax
from jax.experimental import pallas as pl
from jax.experimental.pallas import tpu as pltpu
from jax.sharding import PartitionSpec as P

BF = jnp.bfloat16
F32 = jnp.float32
B = 128
LIMIT = 60 << 20


def split(x):
    h=x.astype(BF); return h,(x-h.astype(F32)).astype(BF)
def rot(h):
    return jnp.concatenate([h, jnp.concatenate([-h[:,128:], h[:,:128]],1)],0)
def dot(a,b): return lax.dot_general(a,b,(((1,),(0,)),((),())),preferred_element_type=F32)
def dott(a,b): return lax.dot_general(a,b,(((1,),(1,)),((),())),preferred_element_type=F32)
def rotT(Tr,Ti):
    return jnp.concatenate([jnp.concatenate([Tr,-Ti],1),jnp.concatenate([Ti,Tr],1)],0)
def term(G,S):
    Gh,Gl=split(jnp.concatenate([G[0],G[1]],1)); Sh,Sl=split(jnp.concatenate([S[0],S[1]],1))
    tr,ti=G[0].T,G[1].T
    trh,trl=split(tr); tih,til=split(ti)
    Wh=rotT(trh,tih); Wl=rotT(trl,til)
    T2=dot(jnp.concatenate([Gh,Gl],0),rot(Sh)); T=T2[:128]+T2[128:]+dot(Gh,rot(Sl))
    Th,Tl=split(T)
    F2=dot(jnp.concatenate([Th,Tl],0),Wh)
    return F2[:128]+F2[128:]+dot(Th,Wl)

def dft_mats():
    a=np.arange(128); th=2*np.pi*((a[:,None]*a[None,:])%128)/128
    C,S=np.cos(th),np.sin(th)
    f=np.block([[C,S],[-S,C]]); b=np.block([[C,-S],[S,C]])
    out=[]
    for m in (f,b):
        h=m.astype(np.float32).astype(BF); l=(m-h.astype(np.float64)).astype(np.float32).astype(BF)
        out.append(np.concatenate([h,l],0))
    return np.stack(out)
def tw_tab():
    a=np.arange(128)[:,None]; p=np.arange(8)[None,:]
    th=2*np.pi*(a*p)/1024
    t=np.zeros((128,128),np.float32); t[:,:8]=np.cos(th); t[:,8:16]=np.sin(th)
    return t

R2=math.sqrt(0.5)
def radix8(x,sign):
    add=lambda u,v:(u[0]+v[0],u[1]+v[1]); sub=lambda u,v:(u[0]-v[0],u[1]-v[1])
    mi=(lambda u:(u[1],-u[0])) if sign<0 else (lambda u:(-u[1],u[0]))
    def r4(y):
        s0,d0=add(y[0],y[2]),sub(y[0],y[2]); s1,d1=add(y[1],y[3]),mi(sub(y[1],y[3]))
        return [add(s0,s1),add(d0,d1),sub(s0,s1),sub(d0,d1)]
    e=r4(x[0::2]); o=r4(x[1::2])
    def w1(u):
        m=mi(u); return ((u[0]+m[0])*R2,(u[1]+m[1])*R2)
    o=[o[0],w1(o[1]),mi(o[2]),w1(mi(o[3]))]
    return [add(e[k],o[k]) for k in range(4)]+[sub(e[k],o[k]) for k in range(4)]
def conv_r(ld_x,ld_s,st_o,scale,tw,dm,yh,yl,v):
    for ch in range(8):
        x=[(ld_x(4*b+ch//2,0,(ch%2)*16),ld_x(4*b+ch//2,1,(ch%2)*16)) for b in range(8)]
        y=radix8(x,-1)
        rs=slice(ch*16,ch*16+16)
        for p in range(8):
            re,im=y[p]
            if p:
                c,s=tw[p,0,rs,:],tw[p,1,rs,:]
                re,im=re*c+im*s,im*c-re*s
            for k,val in enumerate((re,im)):
                h,l=split(val)
                yh[p,k*128+ch*16:k*128+ch*16+16,:]=h; yl[p,k*128+ch*16:k*128+ch*16+16,:]=l
    for pp in range(4):
        p0,p1=2*pp,2*pp+1
        H=jnp.concatenate([yh[p0],yh[p1]],1); L=jnp.concatenate([yl[p0],yl[p1]],1)
        D=dm[0]
        A=dot(D,H); Z=A[:256]+A[256:]+dot(D[:256],L)
        wr=jnp.concatenate([ld_s(p0,0),ld_s(p1,0)],1); wi=jnp.concatenate([ld_s(p0,1),ld_s(p1,1)],1)
        zr,zi=Z[:128],Z[128:]
        Q=jnp.concatenate([zr*wr-zi*wi,zr*wi+zi*wr],0)
        h,l=split(Q)
        D=dm[1]
        A=dot(D,h); V=A[:256]+A[256:]+dot(D[:256],l)
        v[p0]=V[:,:128]; v[p1]=V[:,128:]
    for ch in range(16):
        rs=slice(ch*8,ch*8+8); ri=slice(128+ch*8,128+ch*8+8)
        x=[]
        for p in range(8):
            re,im=v[p,rs,:],v[p,ri,:]
            if p:
                c,s=tw[p,0,rs,:],tw[p,1,rs,:]
                re,im=re*c-im*s,im*c+re*s
            x.append((re,im))
        y=radix8(x,1)
        for b in range(8):
            d=4*b+ch//4
            st_o(d,0,(ch%4)*8,y[b][1]*(-scale)); st_o(d,1,(ch%4)*8,y[b][0]*scale)
def fill_tw(tab,tw):
    for p in range(1,8):
        tw[p,0]=jnp.broadcast_to(tab[:,p:p+1],(128,128)); tw[p,1]=jnp.broadcast_to(tab[:,8+p:9+p],(128,128))

ENERGY = 32
ROWS = 8192
CHUNK = 2048
UNROLL = 8
MESH = pl.DeviceIdType.MESH


def kernel(
    gd_h, gl_h, gu_h, s_h, sc_h, pat, row_on, dm_h, tab_h, out,
    gd, gn, gx, sig, near, cross, obuf, recv, ret, rx, scr, tw, yh, yl, v, dm, tab,
    load_sem, sc_sem, own_sem, n_s, n_r, x_s, x_r,
    a_s, a_r, b_s, b_r, c_s, c_r, n2_s, n2_r, credit,
):
    me = lax.axis_index("energy")
    slab = lax.axis_index("slab")
    odd = lax.rem(slab, 2)
    has_cross = jnp.logical_or(slab == 1, slab == 2)
    near_slab = slab + 1 - 2 * odd
    cross_slab = 3 - slab

    def load(k, j, src, dst):
        at = pl.ds(pl.multiple_of(k * CHUNK, CHUNK), CHUNK)
        return pltpu.make_async_copy(src.at[at], dst.at[at], load_sem.at[j, k])

    sc_copy = pltpu.make_async_copy(sc_h, scr, sc_sem.at[0])
    for k in range(4):
        load(k, 0, s_h, sig).start()
        load(k, 1, gd_h, gd).start()

        @pl.when(odd == 0)
        def _():
            load(k, 2, gu_h, gn).start()
            load(k, 3, gl_h, gx).start()

        @pl.when(odd == 1)
        def _():
            load(k, 2, gl_h, gn).start()
            load(k, 3, gu_h, gx).start()

    sc_copy.start()
    tab_copy = pltpu.make_async_copy(tab_h, tab, sc_sem.at[1])
    dm_copy = pltpu.make_async_copy(dm_h, dm, sc_sem.at[2])
    tab_copy.start()
    dm_copy.start()

    barrier = pltpu.get_barrier_semaphore()
    pl.semaphore_signal(barrier, inc=1, device_id={"slab": near_slab}, device_id_type=MESH)

    @pl.when(has_cross)
    def _():
        def greet_cross(d, carry):
            pl.semaphore_signal(
                barrier, inc=1,
                device_id={"energy": lax.rem(me + d, ENERGY), "slab": cross_slab}, device_id_type=MESH,
            )
            return carry

        lax.fori_loop(0, ENERGY, greet_cross, 0)

    def greet(d, carry):
        pl.semaphore_signal(barrier, inc=1, device_id={"energy": lax.rem(me + d, ENERGY)}, device_id_type=MESH)
        return carry

    lax.fori_loop(1, ENERGY, greet, 0)

    @pl.when(jnp.logical_not(has_cross))
    def _():
        cross[...] = jnp.zeros_like(cross)
        rx[...] = jnp.zeros_like(rx)

    tab_copy.wait()
    fill_tw(tab, tw)
    pl.semaphore_wait(barrier, ENERGY + jnp.where(has_cross, ENERGY, 0))

    def halo(src, k, dst, s_sem, r_sem, to):
        at = pl.ds(pl.multiple_of(k * CHUNK, CHUNK), CHUNK)
        return pltpu.make_async_remote_copy(
            src_ref=src.at[at], dst_ref=dst.at[at], send_sem=s_sem.at[k], recv_sem=r_sem.at[k],
            device_id={"slab": to}, device_id_type=MESH,
        )

    def to_near(k):
        return halo(s_h, k, near, n_s, n_r, near_slab)

    def to_cross(k):
        return halo(s_h, k, cross, x_s, x_r, cross_slab)

    def to_near_again(k):
        return halo(sig, k, near, n2_s, n2_r, near_slab)

    for k in range(4):
        @pl.when(has_cross)
        def _():
            to_cross(k).start()

        to_near(k).start()

    def get(ref, e):
        at = pl.multiple_of(e * 256, 256)
        return ref[pl.ds(at, B), :], ref[pl.ds(at + B, B), :]

    def own_near(e):
        return term(get(gd, e), get(sig, e)) + term(get(gn, e), get(near, e))

    def each(k, body):
        def some(j, carry):
            for u in range(UNROLL):
                body(j * UNROLL + u, k * 8 + j * UNROLL + u)
            return carry

        lax.fori_loop(0, 8 // UNROLL, some, 0)

    def a_copy(k, peer):
        return pltpu.make_async_remote_copy(
            src_ref=obuf.at[pl.ds(pl.multiple_of(k * CHUNK + peer * 64, 64), 64)],
            dst_ref=recv.at[pl.ds(pl.multiple_of(me * 256 + k * 64, 64), 64)],
            send_sem=a_s.at[0], recv_sem=a_r.at[0],
            device_id={"energy": peer}, device_id_type=MESH,
        )

    def a_own(k):
        return pltpu.make_async_copy(
            obuf.at[pl.ds(pl.multiple_of(k * CHUNK + me * 64, 64), 64)],
            recv.at[pl.ds(pl.multiple_of(me * 256 + k * 64, 64), 64)],
            own_sem.at[k],
        )

    def put(ref, e, f):
        at = pl.multiple_of(e * 256, 256)
        ref[pl.ds(at, B), :] = f[:, :B]
        ref[pl.ds(at + B, B), :] = f[:, B:]

    def first_part(k, carry):
        load(k, 0, s_h, sig).wait()
        load(k, 1, gd_h, gd).wait()
        load(k, 2, gu_h, gn).wait()
        to_near(k).wait_recv()
        each(k, lambda e8, e: put(ret, e, own_near(e)))
        return carry

    lax.fori_loop(0, 4, first_part, 0)
    pl.semaphore_signal(credit.at[0], inc=1, device_id={"slab": near_slab}, device_id_type=MESH)

    def first_cross(k, carry):
        load(k, 3, gl_h, gx).wait()

        @pl.when(has_cross)
        def _():
            to_cross(k).wait_recv()

        def add(e8, e):
            f = term(get(gx, e), get(cross, e))
            re, im = get(ret, e)
            obuf[pl.ds(k * CHUNK + e8, B, stride=16), :] = re + f[:, :B]
            obuf[pl.ds(k * CHUNK + 8 + e8, B, stride=16), :] = im + f[:, B:]

        each(k, add)

        def send(d, carry):
            a_copy(k, lax.rem(me + d, ENERGY)).start()
            return carry

        lax.fori_loop(1, ENERGY, send, 0)
        a_own(k).start()
        return carry

    lax.fori_loop(0, 4, first_cross, 0)

    most = pl.ds(0, 31 * 256)
    sc_copy.wait()
    dm_copy.wait()
    for k in range(4):
        a_own(k).wait()
    pltpu.make_async_copy(obuf.at[most], obuf.at[most], a_s.at[0]).wait()
    pltpu.make_async_copy(recv.at[most], recv.at[most], a_r.at[0]).wait()

    def b_copy(k, peer, off, size):
        return pltpu.make_async_remote_copy(
            src_ref=obuf.at[pl.ds(pl.multiple_of(k * CHUNK + peer * 64 + off, 16), size)],
            dst_ref=ret.at[pl.ds(pl.multiple_of(k * CHUNK + me * 64 + off, 16), size)],
            send_sem=b_s.at[0], recv_sem=b_r.at[k],
            device_id={"energy": peer}, device_id_type=MESH,
        )

    def c_copy(k, peer, off, size):
        return pltpu.make_async_remote_copy(
            src_ref=obuf.at[pl.ds(pl.multiple_of(k * CHUNK + peer * 64 + off, 16), size)],
            dst_ref=rx.at[pl.ds(pl.multiple_of(k * CHUNK + me * 64 + off, 16), size)],
            send_sem=c_s.at[0], recv_sem=c_r.at[k],
            device_id={"energy": peer, "slab": cross_slab}, device_id_type=MESH,
        )

    def b_own(k):
        at = pl.ds(pl.multiple_of(k * CHUNK + me * 64, 64), 64)
        return pltpu.make_async_copy(obuf.at[at], ret.at[at], own_sem.at[4 + k])

    def scatter_both(k, off, size):
        def both(d, carry):
            peer = lax.rem(me + d, ENERGY)
            b_copy(k, peer, off, size).start()
            c_copy(k, peer, off, size).start()
            return carry

        lax.fori_loop(1, ENERGY, both, 0)
        c_copy(k, me, off, size).start()

    def scatter_own(k):
        def one(d, carry):
            b_copy(k, lax.rem(me + d, ENERGY), 0, 64).start()
            return carry

        lax.fori_loop(1, ENERGY, one, 0)

    @pl.when(has_cross)
    def _():
        pl.semaphore_signal(credit.at[1], inc=1, device_id={"slab": near_slab}, device_id_type=MESH)

    columns = pat[...].astype(F32)

    def convolve_row(r, carry):
        def ld_x(s, c, r0):
            at = s * 256 + (r0 // 8) * 64 + c * 8
            return jnp.concatenate([
                recv[pl.ds(pl.multiple_of(at + r * 16, 8), 8), :],
                recv[pl.ds(pl.multiple_of(at + 64 + r * 16, 8), 8), :],
            ], 0)

        def ld_s(p, c):
            return scr[pl.ds(p * 8 + c * 4 + r, 128, stride=64), :]

        def st_o(d, c, r0, val):
            at = (r0 // 8) * CHUNK + d * 64 + c * 8
            obuf[pl.ds(pl.multiple_of(at + r * 16, 8), 8), :] = val

        scale = columns * (row_on[0, me * 4 + r].astype(F32) * (1.0 / 1024))
        conv_r(ld_x, ld_s, st_o, scale, tw, dm, yh, yl, v)

        @pl.when(has_cross)
        def _():
            scatter_both(0, r * 16, 16)

        return carry

    lax.fori_loop(0, 4, convolve_row, 0)

    @pl.when(has_cross)
    def _():
        for k in range(1, 4):
            scatter_both(k, 0, 64)

    @pl.when(jnp.logical_not(has_cross))
    def _():
        pl.semaphore_wait(credit.at[1], 1)
        for k in range(4):
            scatter_own(k)

    for k in range(4):
        b_own(k).start()
    pl.semaphore_wait(credit.at[0], 1)

    def update(field, new, k):
        for e8 in range(8):
            at = pl.multiple_of((k * 8 + e8) * 256, 256)
            for c in range(2):
                rows = pl.ds(at + c * B, B)
                field[rows, :] = field[rows, :] + new[pl.ds(k * CHUNK + c * 8 + e8, B, stride=16), :]

    def second_chunk(k, carry):
        at = pl.multiple_of(k * CHUNK, CHUNK)
        part = pl.ds(at, 31 * 64)
        b_own(k).wait()
        pltpu.make_async_copy(ret.at[part], ret.at[part], b_r.at[k]).wait()
        update(sig, ret, k)
        to_near_again(k).start()

        @pl.when(has_cross)
        def _():
            part = pl.ds(at, CHUNK)
            pltpu.make_async_copy(rx.at[part], rx.at[part], c_r.at[k]).wait()

        def own_cross(e8, e):
            re, im = get(cross, e)
            new = [rx[pl.ds(k * CHUNK + c * 8 + e8, B, stride=16), :] for c in range(2)]
            put(recv, e, term(get(gd, e), get(sig, e)) + term(get(gx, e), (re + new[0], im + new[1])))

        each(k, own_cross)
        to_near_again(k).wait_recv()

        def add(e8, e):
            f = term(get(gn, e), get(near, e))
            re, im = get(recv, e)
            put(out, e, jnp.concatenate([re, im], 1) + f)

        each(k, add)
        return carry

    lax.fori_loop(0, 4, second_chunk, 0)
    pltpu.make_async_copy(obuf.at[most], obuf.at[most], b_s.at[0]).wait()

    @pl.when(has_cross)
    def _():
        pltpu.make_async_copy(obuf, obuf, c_s.at[0]).wait()
        for k in range(4):
            to_cross(k).wait_send()

    for k in range(4):
        to_near(k).wait_send()
        to_near_again(k).wait_send()


def local(green_diag, green_lower, green_upper, sigma_lesser, screened, pattern):
    fields = [a.reshape(ROWS, B) for a in (green_diag, green_lower, green_upper, sigma_lesser, screened)]
    hbm = pl.BlockSpec(memory_space=pl.ANY)
    whole = pl.BlockSpec(memory_space=pltpu.VMEM)
    field = pltpu.VMEM((ROWS, B), F32)
    dma = pltpu.SemaphoreType.DMA
    one, four = dma((1,)), dma((4,))
    out = pl.pallas_call(
        kernel,
        out_shape=pltpu.VMEM((ROWS, B), F32),
        in_specs=[hbm] * 5 + [whole, pl.BlockSpec(memory_space=pltpu.SMEM), hbm, hbm],
        out_specs=whole,
        scratch_shapes=[field] * 11 + [
            pltpu.VMEM((8, 2, B, B), F32), pltpu.VMEM((8, 256, B), BF),
            pltpu.VMEM((8, 256, B), BF), pltpu.VMEM((8, 256, B), F32),
            pltpu.VMEM((2, 512, 256), BF), pltpu.VMEM((B, B), F32),
            dma((4, 4)), dma((3,)), dma((8,)), four, four, four, four,
            one, one, one, four, one, four, four, four,
            pltpu.SemaphoreType.REGULAR((2,)),
        ],
        compiler_params=pltpu.CompilerParams(
            vmem_limit_bytes=55 << 20, collective_id=0, has_side_effects=True
        ),
        name="gw",
    )(*fields, pattern, pattern, jnp.asarray(dft_mats()), jnp.asarray(tw_tab()))
    return out.reshape(1, 32, 2, B, B)


def solution(mesh):
    return jax.shard_map(
        local,
        mesh=mesh,
        in_specs=(
            P("slab", "energy", None, None, None),
            P("slab", "energy", None, None, None),
            P("slab", "energy", None, None, None),
            P("slab", "energy", None, None, None),
            P("slab", None, None, "energy", None),
            P("slab", None),
        ),
        out_specs=P("slab", "energy", None, None, None),
        check_vma=False,
    )
```

```python
import functools
import math

import jax
import jax.numpy as jnp
import numpy as np
from jax import lax
from jax.experimental import pallas as pl
from jax.experimental.pallas import tpu as pltpu
from jax.sharding import PartitionSpec as P

BF = jnp.bfloat16
F32 = jnp.float32
B = 128
LIMIT = 60 << 20


def split(x):
    h=x.astype(BF); return h,(x-h.astype(F32)).astype(BF)
def rot(h):
    return jnp.concatenate([h, jnp.concatenate([-h[:,128:], h[:,:128]],1)],0)
def dot(a,b): return lax.dot_general(a,b,(((1,),(0,)),((),())),preferred_element_type=F32)
def dott(a,b): return lax.dot_general(a,b,(((1,),(1,)),((),())),preferred_element_type=F32)
def rotT(Tr,Ti):
    return jnp.concatenate([jnp.concatenate([Tr,-Ti],1),jnp.concatenate([Ti,Tr],1)],0)
def term(G,S):
    Gh,Gl=split(jnp.concatenate([G[0],G[1]],1)); Sh,Sl=split(jnp.concatenate([S[0],S[1]],1))
    tr,ti=G[0].T,G[1].T
    trh,trl=split(tr); tih,til=split(ti)
    Wh=rotT(trh,tih); Wl=rotT(trl,til)
    T2=dot(jnp.concatenate([Gh,Gl],0),rot(Sh)); T=T2[:128]+T2[128:]+dot(Gh,rot(Sl))
    Th,Tl=split(T)
    F2=dot(jnp.concatenate([Th,Tl],0),Wh)
    return F2[:128]+F2[128:]+dot(Th,Wl)

def dft_mats():
    a=np.arange(128); th=2*np.pi*((a[:,None]*a[None,:])%128)/128
    C,S=np.cos(th),np.sin(th)
    f=np.block([[C,S],[-S,C]]); b=np.block([[C,-S],[S,C]])
    out=[]
    for m in (f,b):
        h=m.astype(np.float32).astype(BF); l=(m-h.astype(np.float64)).astype(np.float32).astype(BF)
        out.append(np.concatenate([h,l],0))
    return np.stack(out)
def tw_tab():
    a=np.arange(128)[:,None]; p=np.arange(8)[None,:]
    th=2*np.pi*(a*p)/1024
    t=np.zeros((128,128),np.float32); t[:,:8]=np.cos(th); t[:,8:16]=np.sin(th)
    return t

R2=math.sqrt(0.5)
def radix8(x,sign):
    add=lambda u,v:(u[0]+v[0],u[1]+v[1]); sub=lambda u,v:(u[0]-v[0],u[1]-v[1])
    mi=(lambda u:(u[1],-u[0])) if sign<0 else (lambda u:(-u[1],u[0]))
    def r4(y):
        s0,d0=add(y[0],y[2]),sub(y[0],y[2]); s1,d1=add(y[1],y[3]),mi(sub(y[1],y[3]))
        return [add(s0,s1),add(d0,d1),sub(s0,s1),sub(d0,d1)]
    e=r4(x[0::2]); o=r4(x[1::2])
    def w1(u):
        m=mi(u); return ((u[0]+m[0])*R2,(u[1]+m[1])*R2)
    o=[o[0],w1(o[1]),mi(o[2]),w1(mi(o[3]))]
    return [add(e[k],o[k]) for k in range(4)]+[sub(e[k],o[k]) for k in range(4)]
def conv_r(ld_x,ld_s,st_o,scale,tw,dm,yh,yl,v):
    for ch in range(8):
        x=[(ld_x(4*b+ch//2,0,(ch%2)*16),ld_x(4*b+ch//2,1,(ch%2)*16)) for b in range(8)]
        y=radix8(x,-1)
        rs=slice(ch*16,ch*16+16)
        for p in range(8):
            re,im=y[p]
            if p:
                c,s=tw[p,0,rs,:],tw[p,1,rs,:]
                re,im=re*c+im*s,im*c-re*s
            for k,val in enumerate((re,im)):
                h,l=split(val)
                yh[p,k*128+ch*16:k*128+ch*16+16,:]=h; yl[p,k*128+ch*16:k*128+ch*16+16,:]=l
    for pp in range(4):
        p0,p1=2*pp,2*pp+1
        H=jnp.concatenate([yh[p0],yh[p1]],1); L=jnp.concatenate([yl[p0],yl[p1]],1)
        D=dm[0]
        A=dot(D,H); Z=A[:256]+A[256:]+dot(D[:256],L)
        wr=jnp.concatenate([ld_s(p0,0),ld_s(p1,0)],1); wi=jnp.concatenate([ld_s(p0,1),ld_s(p1,1)],1)
        zr,zi=Z[:128],Z[128:]
        Q=jnp.concatenate([zr*wr-zi*wi,zr*wi+zi*wr],0)
        h,l=split(Q)
        D=dm[1]
        A=dot(D,h); V=A[:256]+A[256:]+dot(D[:256],l)
        v[p0]=V[:,:128]; v[p1]=V[:,128:]
    for ch in range(16):
        rs=slice(ch*8,ch*8+8); ri=slice(128+ch*8,128+ch*8+8)
        x=[]
        for p in range(8):
            re,im=v[p,rs,:],v[p,ri,:]
            if p:
                c,s=tw[p,0,rs,:],tw[p,1,rs,:]
                re,im=re*c-im*s,im*c+re*s
            x.append((re,im))
        y=radix8(x,1)
        for b in range(8):
            d=4*b+ch//4
            st_o(d,0,(ch%4)*8,y[b][1]*(-scale)); st_o(d,1,(ch%4)*8,y[b][0]*scale)
def fill_tw(tab,tw):
    for p in range(1,8):
        tw[p,0]=jnp.broadcast_to(tab[:,p:p+1],(128,128)); tw[p,1]=jnp.broadcast_to(tab[:,8+p:9+p],(128,128))

ENERGY = 32
ROWS = 8192
CHUNK = 2048
UNROLL = 8
MESH = pl.DeviceIdType.MESH


def kernel(
    gd_h, gl_h, gu_h, s_h, sc_h, pat, row_on, dm_h, tab_h, out,
    gd, gn, gx, sig, near, cross, obuf, recv, ret, rx, scr, tw, yh, yl, v, dm, tab,
    load_sem, sc_sem, own_sem, n_s, n_r, x_s, x_r,
    a_s, a_r, b_s, b_r, c_s, c_r, n2_s, n2_r, credit,
):
    me = lax.axis_index("energy")
    slab = lax.axis_index("slab")
    odd = lax.rem(slab, 2)
    has_cross = jnp.logical_or(slab == 1, slab == 2)
    near_slab = slab + 1 - 2 * odd
    cross_slab = 3 - slab

    def load(k, j, src, dst):
        at = pl.ds(pl.multiple_of(k * CHUNK, CHUNK), CHUNK)
        return pltpu.make_async_copy(src.at[at], dst.at[at], load_sem.at[j, k])

    sc_copy = pltpu.make_async_copy(sc_h, scr, sc_sem.at[0])
    for k in range(4):
        load(k, 0, s_h, sig).start()
        load(k, 1, gd_h, gd).start()

        @pl.when(odd == 0)
        def _():
            load(k, 2, gu_h, gn).start()
            load(k, 3, gl_h, gx).start()

        @pl.when(odd == 1)
        def _():
            load(k, 2, gl_h, gn).start()
            load(k, 3, gu_h, gx).start()

    sc_copy.start()
    tab_copy = pltpu.make_async_copy(tab_h, tab, sc_sem.at[1])
    dm_copy = pltpu.make_async_copy(dm_h, dm, sc_sem.at[2])
    tab_copy.start()
    dm_copy.start()

    barrier = pltpu.get_barrier_semaphore()
    pl.semaphore_signal(barrier, inc=1, device_id={"slab": near_slab}, device_id_type=MESH)

    @pl.when(has_cross)
    def _():
        def greet_cross(d, carry):
            pl.semaphore_signal(
                barrier, inc=1,
                device_id={"energy": lax.rem(me + d, ENERGY), "slab": cross_slab}, device_id_type=MESH,
            )
            return carry

        lax.fori_loop(0, ENERGY, greet_cross, 0)

    def greet(d, carry):
        pl.semaphore_signal(barrier, inc=1, device_id={"energy": lax.rem(me + d, ENERGY)}, device_id_type=MESH)
        return carry

    lax.fori_loop(1, ENERGY, greet, 0)

    @pl.when(jnp.logical_not(has_cross))
    def _():
        cross[...] = jnp.zeros_like(cross)
        rx[...] = jnp.zeros_like(rx)

    tab_copy.wait()
    fill_tw(tab, tw)
    pl.semaphore_wait(barrier, ENERGY + jnp.where(has_cross, ENERGY, 0))

    def halo(src, k, dst, s_sem, r_sem, to):
        at = pl.ds(pl.multiple_of(k * CHUNK, CHUNK), CHUNK)
        return pltpu.make_async_remote_copy(
            src_ref=src.at[at], dst_ref=dst.at[at], send_sem=s_sem.at[k], recv_sem=r_sem.at[k],
            device_id={"slab": to}, device_id_type=MESH,
        )

    def to_near(k):
        return halo(s_h, k, near, n_s, n_r, near_slab)

    def to_cross(k):
        return halo(s_h, k, cross, x_s, x_r, cross_slab)

    def to_near_again(k):
        return halo(sig, k, near, n2_s, n2_r, near_slab)

    for k in range(4):
        @pl.when(has_cross)
        def _():
            to_cross(k).start()

        to_near(k).start()

    def get(ref, e):
        at = pl.multiple_of(e * 256, 256)
        return ref[pl.ds(at, B), :], ref[pl.ds(at + B, B), :]

    def own_near(e):
        return term(get(gd, e), get(sig, e)) + term(get(gn, e), get(near, e))

    def each(k, body):
        def some(j, carry):
            for u in range(UNROLL):
                body(j * UNROLL + u, k * 8 + j * UNROLL + u)
            return carry

        lax.fori_loop(0, 8 // UNROLL, some, 0)

    def a_copy(k, peer):
        return pltpu.make_async_remote_copy(
            src_ref=obuf.at[pl.ds(pl.multiple_of(k * CHUNK + peer * 64, 64), 64)],
            dst_ref=recv.at[pl.ds(pl.multiple_of(me * 256 + k * 64, 64), 64)],
            send_sem=a_s.at[0], recv_sem=a_r.at[0],
            device_id={"energy": peer}, device_id_type=MESH,
        )

    def a_own(k):
        return pltpu.make_async_copy(
            obuf.at[pl.ds(pl.multiple_of(k * CHUNK + me * 64, 64), 64)],
            recv.at[pl.ds(pl.multiple_of(me * 256 + k * 64, 64), 64)],
            own_sem.at[k],
        )

    def put(ref, e, f):
        at = pl.multiple_of(e * 256, 256)
        ref[pl.ds(at, B), :] = f[:, :B]
        ref[pl.ds(at + B, B), :] = f[:, B:]

    def first_part(k, carry):
        load(k, 0, s_h, sig).wait()
        load(k, 1, gd_h, gd).wait()
        load(k, 2, gu_h, gn).wait()
        to_near(k).wait_recv()
        each(k, lambda e8, e: put(ret, e, own_near(e)))
        return carry

    lax.fori_loop(0, 4, first_part, 0)
    pl.semaphore_signal(credit.at[0], inc=1, device_id={"slab": near_slab}, device_id_type=MESH)

    def first_cross(k, carry):
        load(k, 3, gl_h, gx).wait()

        @pl.when(has_cross)
        def _():
            to_cross(k).wait_recv()

        def add(e8, e):
            f = term(get(gx, e), get(cross, e))
            re, im = get(ret, e)
            obuf[pl.ds(k * CHUNK + e8, B, stride=16), :] = re + f[:, :B]
            obuf[pl.ds(k * CHUNK + 8 + e8, B, stride=16), :] = im + f[:, B:]

        each(k, add)

        def send(d, carry):
            a_copy(k, lax.rem(me + d, ENERGY)).start()
            return carry

        lax.fori_loop(1, ENERGY, send, 0)
        a_own(k).start()
        return carry

    lax.fori_loop(0, 4, first_cross, 0)

    most = pl.ds(0, 31 * 256)
    sc_copy.wait()
    dm_copy.wait()
    for k in range(4):
        a_own(k).wait()
    pltpu.make_async_copy(obuf.at[most], obuf.at[most], a_s.at[0]).wait()
    pltpu.make_async_copy(recv.at[most], recv.at[most], a_r.at[0]).wait()

    def b_copy(k, peer, off, size):
        return pltpu.make_async_remote_copy(
            src_ref=obuf.at[pl.ds(pl.multiple_of(k * CHUNK + peer * 64 + off, 16), size)],
            dst_ref=ret.at[pl.ds(pl.multiple_of(k * CHUNK + me * 64 + off, 16), size)],
            send_sem=b_s.at[0], recv_sem=b_r.at[k],
            device_id={"energy": peer}, device_id_type=MESH,
        )

    def c_copy(k, peer, off, size):
        return pltpu.make_async_remote_copy(
            src_ref=obuf.at[pl.ds(pl.multiple_of(k * CHUNK + peer * 64 + off, 16), size)],
            dst_ref=rx.at[pl.ds(pl.multiple_of(k * CHUNK + me * 64 + off, 16), size)],
            send_sem=c_s.at[0], recv_sem=c_r.at[k],
            device_id={"energy": peer, "slab": cross_slab}, device_id_type=MESH,
        )

    def b_own(k):
        at = pl.ds(pl.multiple_of(k * CHUNK + me * 64, 64), 64)
        return pltpu.make_async_copy(obuf.at[at], ret.at[at], own_sem.at[4 + k])

    def scatter_both(k, off, size):
        def both(d, carry):
            peer = lax.rem(me + d, ENERGY)
            b_copy(k, peer, off, size).start()
            c_copy(k, lax.rem(peer + 16, ENERGY), off, size).start()
            return carry

        lax.fori_loop(1, ENERGY, both, 0)
        c_copy(k, lax.rem(me + 16, ENERGY), off, size).start()

    def scatter_own(k):
        def one(d, carry):
            b_copy(k, lax.rem(me + d, ENERGY), 0, 64).start()
            return carry

        lax.fori_loop(1, ENERGY, one, 0)

    @pl.when(has_cross)
    def _():
        pl.semaphore_signal(credit.at[1], inc=1, device_id={"slab": near_slab}, device_id_type=MESH)

    columns = pat[...].astype(F32)

    def convolve_row(r, carry):
        def ld_x(s, c, r0):
            at = s * 256 + (r0 // 8) * 64 + c * 8
            return jnp.concatenate([
                recv[pl.ds(pl.multiple_of(at + r * 16, 8), 8), :],
                recv[pl.ds(pl.multiple_of(at + 64 + r * 16, 8), 8), :],
            ], 0)

        def ld_s(p, c):
            return scr[pl.ds(p * 8 + c * 4 + r, 128, stride=64), :]

        def st_o(d, c, r0, val):
            at = (r0 // 8) * CHUNK + d * 64 + c * 8
            obuf[pl.ds(pl.multiple_of(at + r * 16, 8), 8), :] = val

        scale = columns * (row_on[0, me * 4 + r].astype(F32) * (1.0 / 1024))
        conv_r(ld_x, ld_s, st_o, scale, tw, dm, yh, yl, v)

        @pl.when(has_cross)
        def _():
            scatter_both(0, r * 16, 16)

        return carry

    lax.fori_loop(0, 4, convolve_row, 0)

    @pl.when(has_cross)
    def _():
        for k in range(1, 4):
            scatter_both(k, 0, 64)

    @pl.when(jnp.logical_not(has_cross))
    def _():
        pl.semaphore_wait(credit.at[1], 1)
        for k in range(4):
            scatter_own(k)

    for k in range(4):
        b_own(k).start()
    pl.semaphore_wait(credit.at[0], 1)

    def update(field, new, k):
        for e8 in range(8):
            at = pl.multiple_of((k * 8 + e8) * 256, 256)
            for c in range(2):
                rows = pl.ds(at + c * B, B)
                field[rows, :] = field[rows, :] + new[pl.ds(k * CHUNK + c * 8 + e8, B, stride=16), :]

    def second_chunk(k, carry):
        at = pl.multiple_of(k * CHUNK, CHUNK)
        part = pl.ds(at, 31 * 64)
        b_own(k).wait()
        pltpu.make_async_copy(ret.at[part], ret.at[part], b_r.at[k]).wait()
        update(sig, ret, k)
        to_near_again(k).start()

        @pl.when(has_cross)
        def _():
            part = pl.ds(at, CHUNK)
            pltpu.make_async_copy(rx.at[part], rx.at[part], c_r.at[k]).wait()

        def own_cross(e8, e):
            re, im = get(cross, e)
            new = [rx[pl.ds(k * CHUNK + c * 8 + e8, B, stride=16), :] for c in range(2)]
            put(recv, e, term(get(gd, e), get(sig, e)) + term(get(gx, e), (re + new[0], im + new[1])))

        each(k, own_cross)
        to_near_again(k).wait_recv()

        def add(e8, e):
            f = term(get(gn, e), get(near, e))
            re, im = get(recv, e)
            put(out, e, jnp.concatenate([re, im], 1) + f)

        each(k, add)
        return carry

    lax.fori_loop(0, 4, second_chunk, 0)
    pltpu.make_async_copy(obuf.at[most], obuf.at[most], b_s.at[0]).wait()

    @pl.when(has_cross)
    def _():
        pltpu.make_async_copy(obuf, obuf, c_s.at[0]).wait()
        for k in range(4):
            to_cross(k).wait_send()

    for k in range(4):
        to_near(k).wait_send()
        to_near_again(k).wait_send()


def local(green_diag, green_lower, green_upper, sigma_lesser, screened, pattern):
    fields = [a.reshape(ROWS, B) for a in (green_diag, green_lower, green_upper, sigma_lesser, screened)]
    hbm = pl.BlockSpec(memory_space=pl.ANY)
    whole = pl.BlockSpec(memory_space=pltpu.VMEM)
    field = pltpu.VMEM((ROWS, B), F32)
    dma = pltpu.SemaphoreType.DMA
    one, four = dma((1,)), dma((4,))
    out = pl.pallas_call(
        kernel,
        out_shape=pltpu.VMEM((ROWS, B), F32),
        in_specs=[hbm] * 5 + [whole, pl.BlockSpec(memory_space=pltpu.SMEM), hbm, hbm],
        out_specs=whole,
        scratch_shapes=[field] * 11 + [
            pltpu.VMEM((8, 2, B, B), F32), pltpu.VMEM((8, 256, B), BF),
            pltpu.VMEM((8, 256, B), BF), pltpu.VMEM((8, 256, B), F32),
            pltpu.VMEM((2, 512, 256), BF), pltpu.VMEM((B, B), F32),
            dma((4, 4)), dma((3,)), dma((8,)), four, four, four, four,
            one, one, one, four, one, four, four, four,
            pltpu.SemaphoreType.REGULAR((2,)),
        ],
        compiler_params=pltpu.CompilerParams(
            vmem_limit_bytes=55 << 20, collective_id=0, has_side_effects=True
        ),
        name="gw",
    )(*fields, pattern, pattern, jnp.asarray(dft_mats()), jnp.asarray(tw_tab()))
    return out.reshape(1, 32, 2, B, B)


def solution(mesh):
    return jax.shard_map(
        local,
        mesh=mesh,
        in_specs=(
            P("slab", "energy", None, None, None),
            P("slab", "energy", None, None, None),
            P("slab", "energy", None, None, None),
            P("slab", "energy", None, None, None),
            P("slab", None, None, "energy", None),
            P("slab", None),
        ),
        out_specs=P("slab", "energy", None, None, None),
        check_vma=False,
    )
```
